32 devices in a mesh: bulk: 4 (over y, x), cuts: 8 (over z, core).
Axes of the slice: x: 2, y: 2, z: 4, core: 2. Of those that a mesh axis runs over, the one named last changes fastest.
Arguments:
- amplitudes: bfloat16 [16384, 8192], P('bulk', 'cuts'), may hold values from -6 to 6
- amp_tiles: int32 [128, 64], P('bulk', 'cuts'), may hold values from 0 to 1, as said below
- occ_coupling: bfloat16 [128, 128], replicated, may hold values from -0.5 to 0.5
- integrals: bfloat16 [8192, 2048], P('cuts'), may hold values from -0.09375 to 0.09375
- int_tiles: int32 [64, 16], P('cuts'), may hold values from 0 to 1, as said below
Outputs:
- residual: bfloat16 [2048, 16384], P('cuts', 'bulk')
The draws below stay inside these ranges and needn't reach their ends.
Inputs may be any that keep to these rules, and one draw needn't show every extreme that they name: `amp_tiles`: 1 where a tile is kept; kept tiles follow the distance, round a cycle of fragments, between the fragments of the two tile indices: each row of tiles keeps a band of columns near its own fragment and one near the fragment opposite on the cycle, whose width varies from group to group of rows. `int_tiles`: 1 where a tile is kept; kept tiles follow the distance, round a cycle of fragments, between the fragments of the two tile indices: each row of tiles keeps a band of columns near its own fragment and one near the fragment opposite on the cycle, whose width varies from group to group of rows.
All inputs are finite; a program needn't handle non-finite values.
Results may differ from the reference program's by a relative error of at most 0.0095.
Values may be sent and summed in bfloat16 or wider, within the bound.
A program may use at most 128 MiB of HBM per device.

```python
import jax
import jax.numpy as jnp
from jax import lax

TILE = 128
OCC = 128
CD_DEV = 1024
NO = 16384
NV = 8192
NA = 2048
N_CUTS = 8


def locality(key, rows, cols, salt):
    first, second, third = jax.random.split(jax.random.fold_in(key, salt), 3)
    row_pos = jnp.arange(rows, dtype=jnp.int32) * 64 // rows + jax.random.randint(first, (rows,), -2, 3)
    col_pos = jnp.arange(cols, dtype=jnp.int32) * 64 // cols + jax.random.randint(second, (cols,), -2, 3)
    group = jnp.arange(rows, dtype=jnp.int32) * 16 // rows
    widths = jax.random.randint(third, (16,), 1, 12)[group]
    apart = jnp.mod(row_pos[:, None] - col_pos[None, :] + 128, 64)
    circle = jnp.minimum(apart, 64 - apart)
    near = circle <= widths[:, None]
    across = jnp.abs(circle - 32) <= widths[:, None]
    return jnp.logical_or(near, across).astype(jnp.int32)


def draw_amp_tiles(key, part):
    return locality(key, NO // TILE, NV // TILE, 11)


def draw_int_tiles(key, part):
    return locality(key, NV // TILE, NA // TILE, 23)


def with_spikes(values, own_key, source, target, shards_of, factor):
    owner, partner = [(jnp.arange(values.shape[position]) // (values.shape[position] // shards_of)).reshape([-1 if axis == position else 1 for axis in range(values.ndim)]) for position in (source, target)]
    chosen = jax.random.permutation(own_key, shards_of)[partner]
    strong = (owner == chosen) | (owner == (partner + shards_of // 2) % shards_of)
    return jnp.where(strong, factor * values, values)


def level_of(key, extent, cuts, least, high):
    factor_of, own = 1.0, jax.random.fold_in(key, 6)
    for axis_at, shards_of in cuts:
        draws = jnp.exp(jax.random.uniform(jax.random.fold_in(own, axis_at), (shards_of,), jnp.float32, least / len(cuts), high / len(cuts)))
        factor_of = factor_of * jnp.repeat(draws, extent[axis_at] // shards_of).reshape([-1 if axis == axis_at else 1 for axis in range(len(extent))])
    return factor_of


def bell_draw(rng, shape, deviation, bound, shards=(), kind=jnp.bfloat16):
    factor_of = level_of(rng, shape, shards, -0.22, 0.18) if shards else 1.0
    entries = jax.random.normal(rng, shape, jnp.float32) * deviation * factor_of
    return jnp.minimum(jnp.maximum(entries, -bound), bound).astype(kind)


def noise_with(key, shape, scale, reach, pieces, heavy, held_as=jnp.bfloat16):
    entries = scale * jax.random.normal(key, shape, jnp.float32)
    if pieces:
        entries = entries * level_of(key, shape, pieces, -0.22, 0.18)
    return jnp.clip(with_spikes(entries, jax.random.fold_in(key, 3), *heavy), -reach, reach).astype(held_as)


def setup_inputs(seed: int = 0) -> dict:
    key_of = jax.random.split(jax.random.key(seed), 6)
    return {
        "amplitudes": bell_draw(key_of[0], (NO, NV), 1.0, 6.0, ((0, 4), (1, 8))),
        "amp_tiles": draw_amp_tiles(jax.random.fold_in(key_of[5], 71), 0),
        "occ_coupling": bell_draw(key_of[2], (OCC, OCC), OCC ** -0.5, 0.5),
        "integrals": noise_with(key_of[3], (NV, NA), NV ** -0.5, 0.09375, ((0, 8),), (0, 1, 8, 2.0)),
        "int_tiles": draw_int_tiles(jax.random.fold_in(key_of[5], 71), 0),
    }


def keep_tiles(values, tiles):
    height, width = values.shape
    blocks = values.reshape(height // TILE, TILE, width // TILE, TILE)
    kept = blocks * tiles.astype(values.dtype)[:, None, :, None]
    return kept.reshape(height, width)


def reference(amplitudes, amp_tiles, occ_coupling, integrals, int_tiles):
    amp_kept = keep_tiles(amplitudes, amp_tiles)
    int_kept = keep_tiles(integrals, int_tiles)
    pairs_v = amp_kept.shape[1]
    by_second = amp_kept.reshape(OCC, OCC, pairs_v).transpose(1, 0, 2)

    def dress_slab(slab):
        mixed = jnp.dot(occ_coupling, slab, preferred_element_type=jnp.float32)
        return (slab.astype(jnp.float32) + mixed).astype(jnp.bfloat16)

    dressed = lax.map(dress_slab, by_second).transpose(1, 0, 2).reshape(OCC * OCC, pairs_v)
    tau = keep_tiles(dressed, amp_tiles)
    tau_blocks = tau.reshape(OCC * OCC, N_CUTS, CD_DEV).transpose(1, 0, 2)
    int_blocks = int_kept.reshape(N_CUTS, CD_DEV, int_kept.shape[1])

    def add_block(total, pair):
        tau_b, int_b = pair
        part = lax.dot_general(int_b, tau_b, (((0,), (1,)), ((), ())), preferred_element_type=jnp.float32)
        part = lax.optimization_barrier(part.astype(jnp.bfloat16)).astype(jnp.float32)
        return total + part, None

    start = jnp.zeros((int_kept.shape[1], OCC * OCC), jnp.float32)
    total, unused = lax.scan(add_block, start, (tau_blocks, int_blocks))
    return total.astype(jnp.bfloat16)
```

```python
import functools

import jax
import jax.numpy as jnp
from jax import lax
from jax.experimental import pallas as pl
from jax.experimental.pallas import tpu as pltpu
from jax.sharding import PartitionSpec as P

TILE = 128
CORES = 2
PAIR = 2
MESH = pl.DeviceIdType.MESH
F32 = jnp.float32
BF16 = jnp.bfloat16


def dot(a, b):
    return jnp.dot(a, b, preferred_element_type=F32)


def iota(shape, axis):
    return lax.broadcasted_iota(jnp.int32, shape, axis)


def one_hot(condition):
    return jnp.where(condition, 1.0, 0.0).astype(BF16)


def residual_kernel(
    sizes,
    amp_hbm,
    tiles_ref,
    occ_ref,
    int_hbm,
    int_tiles_ref,
    out_hbm,
    x_buf,
    send_buf,
    slab,
    tau,
    mask,
    map_send,
    map_recv,
    ints,
    part,
    inbox,
    acc,
    c_send,
    c_recv,
    gathered,
    split_rows,
    join_rows,
    mix,
    x_sem,
    own_sem,
    a_send_sem,
    a_recv_sem,
    map_send_sem,
    map_recv_sem,
    int_local_sem,
    int_send_sem,
    int_recv_sem,
    z_send_sem,
    right_sem,
    left_sem,
    c_own_sem,
    c_send_sem,
    c_recv_sem,
    out_sem,
):
    bulk, depth, chunks, firsts, seconds, cols, width, sub_i, sub_j = sizes
    group = bulk * CORES
    rows = slab.shape[1]
    half = width // CORES
    block = firsts * PAIR
    b = lax.axis_index("bulk")
    cut = lax.axis_index("cuts")
    z = cut // CORES
    core = cut % CORES
    me = b * CORES + core

    def at_rank(rank):
        return (rank // CORES, z * CORES + rank % CORES)

    def along(zz):
        return (b, zz * CORES + core)

    def each_peer(body):
        def step(k, carry):
            body((me + k) % group)
            return carry

        lax.fori_loop(1, group, step, 0)

    def x_copy(n):
        return pltpu.make_async_copy(
            amp_hbm.at[:, pl.ds(pl.multiple_of(n * seconds, seconds), seconds), :],
            x_buf.at[n % 2],
            x_sem.at[n % 2],
        )

    def place(n, rank):
        return slab.at[
            n,
            pl.ds(pl.multiple_of((rank // CORES) * block, block), block),
            pl.ds(pl.multiple_of((rank % CORES) * cols, cols), cols),
        ]

    def a_copy(n, to, source):
        return pltpu.make_async_remote_copy(
            src_ref=send_buf.at[n % 2, to],
            dst_ref=place(n, source),
            send_sem=a_send_sem.at[n, to],
            recv_sem=a_recv_sem.at[n, source],
            device_id=at_rank(to),
            device_id_type=MESH,
        )

    def own_copy(n):
        return pltpu.make_async_copy(send_buf.at[n % 2, me], place(n, me), own_sem.at[n % 2])

    def map_copy(to, source):
        return pltpu.make_async_remote_copy(
            src_ref=map_send,
            dst_ref=map_recv.at[
                pl.ds(pl.multiple_of((source // CORES) * firsts, firsts), firsts),
                pl.ds(pl.multiple_of((source % CORES) * TILE, TILE), TILE),
            ],
            send_sem=map_send_sem.at[to],
            recv_sem=map_recv_sem.at[source],
            device_id=at_rank(to),
            device_id_type=MESH,
        )

    def int_rows(which):
        return pl.ds(pl.multiple_of(which * cols, cols), cols)

    def int_local(d):
        return pltpu.make_async_copy(
            int_hbm.at[:, pl.ds(d * width, width)], ints.at[d, int_rows(core), :], int_local_sem.at[d]
        )

    def int_copy(source):
        return pltpu.make_async_remote_copy(
            src_ref=ints.at[:, int_rows(core), :],
            dst_ref=ints.at[:, int_rows(source), :],
            send_sem=int_send_sem,
            recv_sem=int_recv_sem,
            device_id=(b, z * CORES + 1 - core),
            device_id_type=MESH,
        )

    def right_copy(n, d):
        return pltpu.make_async_remote_copy(
            src_ref=part.at[n, d],
            dst_ref=inbox.at[n, d],
            send_sem=z_send_sem.at[n, d],
            recv_sem=right_sem.at[n, d],
            device_id=along((z + 1) % depth),
            device_id_type=MESH,
        )

    def left_copy(n, d, slot):
        return pltpu.make_async_remote_copy(
            src_ref=part.at[n, d],
            dst_ref=inbox.at[n, slot],
            send_sem=z_send_sem.at[n, d],
            recv_sem=left_sem.at[n, d],
            device_id=along((z + depth - 1) % depth),
            device_id_type=MESH,
        )

    def left_slot(d, where):
        return jnp.where(d == where, depth, d)

    def c_copy(n, to, source):
        return pltpu.make_async_remote_copy(
            src_ref=c_send.at[
                n,
                pl.ds(pl.multiple_of((to // CORES) * block, block), block),
                pl.ds(pl.multiple_of((to % CORES) * half, half), half),
            ],
            dst_ref=c_recv.at[n, source],
            send_sem=c_send_sem.at[n, to],
            recv_sem=c_recv_sem.at[n, source],
            device_id=at_rank(to),
            device_id_type=MESH,
        )

    def c_own(n):
        return pltpu.make_async_copy(
            c_send.at[
                n,
                pl.ds(pl.multiple_of(b * block, block), block),
                pl.ds(pl.multiple_of(core * half, half), half),
            ],
            c_recv.at[n, me],
            c_own_sem.at[n],
        )

    def out_copy(n):
        span = pl.ds(pl.multiple_of(n * seconds, seconds), seconds)
        return pltpu.make_async_copy(gathered.at[:, span, :], out_hbm.at[:, span, :], out_sem.at[n])

    def prepare(n):
        x_copy(n).wait()
        for gi in range(firsts // sub_i):
            for gj in range(seconds // sub_j):
                x = x_buf[n % 2, gi * sub_i : (gi + 1) * sub_i, gj * sub_j : (gj + 1) * sub_j, :]
                y = dot(split_rows[...], x.reshape(sub_i * sub_j, cols)).astype(BF16)
                send_buf[
                    n % 2,
                    gj * sub_j // PAIR : (gj + 1) * sub_j // PAIR,
                    gi * sub_i * PAIR : (gi + 1) * sub_i * PAIR,
                    :,
                ] = y.reshape(sub_j // PAIR, sub_i * PAIR, cols)

        @pl.when(n + 2 < chunks)
        def _():
            x_copy(n + 2).start()

    def send_amplitudes(n):
        each_peer(lambda to: a_copy(n, to, me).start())
        own_copy(n).start()

    def dress(n):
        span = min(512, CORES * cols)
        for at in range(0, CORES * cols, span):
            kept = mask[:, at : at + span]
            masked = slab[n, :, at : at + span] * kept
            mixed = dot(mix[...], masked)
            dressed = (masked.astype(F32) + mixed).astype(BF16)
            tau[:, at : at + span] = dressed * kept

    x_copy(0).start()
    if chunks > 1:
        x_copy(1).start()
    for d in range(depth):
        int_local(d).start()

    barrier = pltpu.get_barrier_semaphore()

    def greet(device):
        pl.semaphore_signal(barrier, inc=1, device_id=device, device_id_type=MESH)

    each_peer(lambda to: greet(at_rank(to)))
    pl.when(z > 0)(lambda: greet(along(z - 1)))
    pl.when(z < depth - 1)(lambda: greet(along(z + 1)))

    count = sub_i * sub_j
    r, c = iota((count, count), 0), iota((count, count), 1)
    natural = ((r // PAIR) % sub_i) * sub_j + (r // (PAIR * sub_i)) * PAIR + r % PAIR
    split_rows[...] = one_hot(c == natural)
    natural = ((c // PAIR) % sub_i) * sub_j + (c // (PAIR * sub_i)) * PAIR + c % PAIR
    join_rows[...] = one_hot(r == natural)
    prepare(0)
    tiles = tiles_ref[...].astype(F32)
    map_send[...] = jnp.concatenate(
        [tiles, jnp.zeros((firsts, TILE - tiles.shape[1]), F32)], axis=1
    )

    ends = jnp.where(z > 0, 1, 0) + jnp.where(z < depth - 1, 1, 0)
    pl.semaphore_wait(barrier, group - 1 + ends)

    each_peer(lambda to: map_copy(to, me).start())
    send_amplitudes(0)
    own_map = pltpu.make_async_copy(
        map_send,
        map_recv.at[
            pl.ds(pl.multiple_of(b * firsts, firsts), firsts),
            pl.ds(pl.multiple_of(core * TILE, TILE), TILE),
        ],
        map_recv_sem.at[me],
    )
    own_map.start()

    per_tile = width // TILE
    for d in range(depth):
        int_local(d).wait()
        int_tiles = int_tiles_ref[:, d * per_tile : (d + 1) * per_tile].astype(BF16)
        spread = one_hot(iota((per_tile, width), 1) // TILE == iota((per_tile, width), 0))
        kept = dot(int_tiles, spread).astype(BF16)
        for k in range(cols // TILE):
            span = pl.ds(pl.multiple_of(core * cols + k * TILE, TILE), TILE)
            ints[d, span, :] = ints[d, span, :] * kept[k : k + 1, :]
    int_copy(core).start()

    occ_all = occ_ref.shape[0]
    tall = one_hot(iota((rows, occ_all), 0) // PAIR == iota((rows, occ_all), 1))
    wide = one_hot(iota((occ_all, rows), 1) // PAIR == iota((occ_all, rows), 0))
    stretched = dot(dot(tall, occ_ref[...]).astype(BF16), wide)
    same = iota((rows, rows), 0) % PAIR == iota((rows, rows), 1) % PAIR
    mix[...] = jnp.where(same, stretched, 0.0).astype(BF16)
    if chunks > 1:
        prepare(1)

    own_map.wait()
    each_peer(lambda source: map_copy(source, source).wait_recv())
    tiles_all = dot(tall, map_recv[...].astype(BF16)).astype(BF16)
    lane = iota((CORES * TILE, CORES * cols), 0)
    col = iota((CORES * TILE, CORES * cols), 1)
    mask[...] = dot(
        tiles_all, one_hot(lane == (col // cols) * TILE + (col % cols) // TILE)
    ).astype(BF16)
    int_copy(1 - core).wait_recv()

    farther = jnp.maximum(z, depth - 1 - z)

    def add_into(n, d, slot):
        part[n, d] = (part[n, d].astype(F32) + inbox[n, slot].astype(F32)).astype(BF16)

    def step(t, carry):
        @pl.when(t < chunks)
        def _():
            own_copy(t).wait()
            each_peer(lambda source: a_copy(t, source, source).wait_recv())
            pl.when(t + 1 < chunks)(lambda: send_amplitudes(t + 1))
            dress(t)

            def ladder(k, carry):
                d = jnp.where(z * 2 < depth, depth - 1 - k, k)
                part[t, d] = dot(tau[...], ints[d]).astype(BF16)
                pl.when((z == 0) & (d > 0))(lambda: right_copy(t, d).start())
                pl.when((z == depth - 1) & (d < depth - 1))(
                    lambda: left_copy(t, d, left_slot(d, z - 1)).start()
                )
                return carry

            lax.fori_loop(0, depth, ladder, 0)
            each_peer(lambda to: a_copy(t, to, me).wait_send())
            pl.when(t + 2 < chunks)(lambda: prepare(t + 2))

        m = t - z

        @pl.when((z > 0) & (m >= 0) & (m < chunks))
        def _():
            def pass_on(k, carry):
                d = depth - 1 - k
                right_copy(m, d).wait_recv()
                add_into(m, d, d)
                right_copy(m, d).start()
                return carry

            lax.fori_loop(0, depth - 1 - z, pass_on, 0)

        m_left = t - (depth - 1 - z)

        @pl.when((z < depth - 1) & (m_left >= 0) & (m_left < chunks))
        def _():
            def pass_on(d, carry):
                left_copy(m_left, d, d).wait_recv()
                add_into(m_left, d, d)
                left_copy(m_left, d, left_slot(d, z - 1)).start()
                return carry

            lax.fori_loop(0, z, pass_on, 0)

        m_last = t - farther

        @pl.when((m_last >= 0) & (m_last < chunks))
        def _():
            acc[...] = part[m_last, z].astype(F32)

            @pl.when(z > 0)
            def _():
                right_copy(m_last, z).wait_recv()
                acc[...] += inbox[m_last, z].astype(F32)

            @pl.when(z < depth - 1)
            def _():
                left_copy(m_last, z, depth).wait_recv()
                acc[...] += inbox[m_last, depth].astype(F32)

            c_send[m_last] = acc[...].astype(BF16)
            each_peer(lambda to: c_copy(m_last, to, me).start())
            c_own(m_last).start()

        m_out = t - farther - 1

        @pl.when((m_out >= 0) & (m_out < chunks))
        def _():
            c_own(m_out).wait()
            each_peer(lambda source: c_copy(m_out, source, source).wait_recv())
            for gi in range(firsts // sub_i):
                for gj in range(seconds // sub_j):
                    x = c_recv[
                        m_out,
                        gj * sub_j // PAIR : (gj + 1) * sub_j // PAIR,
                        gi * sub_i * PAIR : (gi + 1) * sub_i * PAIR,
                        :,
                    ]
                    y = dot(join_rows[...], x.reshape(count, half)).astype(BF16)
                    start = pl.multiple_of(m_out * seconds + gj * sub_j, sub_j)
                    gathered[gi * sub_i : (gi + 1) * sub_i, pl.ds(start, sub_j), :] = y.reshape(
                        sub_i, sub_j, half
                    )
            out_copy(m_out).start()

        return carry

    lax.fori_loop(0, chunks + depth, step, 0)

    each_peer(lambda to: map_copy(to, me).wait_send())
    int_copy(core).wait_send()

    def finish(n, carry):
        def sent(d, carry):
            pl.when(d != z)(lambda: right_copy(n, d).wait_send())
            return carry

        lax.fori_loop(0, depth, sent, 0)
        each_peer(lambda to: c_copy(n, to, me).wait_send())
        out_copy(n).wait()
        return carry

    lax.fori_loop(0, chunks, finish, 0)


def transpose_kernel(x_ref, o_ref):
    for k in range(x_ref.shape[0]):
        span = x_ref.shape[1]
        o_ref[:, k * span : (k + 1) * span] = x_ref[k].T


def shards(mesh_shape, amplitudes, amp_tiles, occ_coupling, integrals, int_tiles):
    bulk, cuts = mesh_shape
    depth = cuts // CORES
    group = bulk * CORES
    local_rows, cols = amplitudes.shape
    occ_all = occ_coupling.shape[0]
    firsts = local_rows // occ_all
    seconds = PAIR * group
    chunks = occ_all // seconds
    total = integrals.shape[1]
    width = total // depth
    half = width // CORES
    rows = PAIR * occ_all
    sub_j = min(seconds, max(16, 256 // firsts))
    sub_i = min(firsts, 256 // sub_j)
    count = sub_i * sub_j
    sizes = (bulk, depth, chunks, firsts, seconds, cols, width, sub_i, sub_j)
    vmem, dma = pltpu.VMEM, pltpu.SemaphoreType.DMA
    any_space = pl.BlockSpec(memory_space=pl.ANY)
    in_vmem = pl.BlockSpec(memory_space=pltpu.VMEM)
    gathered = pl.pallas_call(
        functools.partial(residual_kernel, sizes),
        out_shape=jax.ShapeDtypeStruct((firsts, occ_all, half), BF16),
        in_specs=[any_space, in_vmem, in_vmem, any_space, in_vmem],
        out_specs=any_space,
        scratch_shapes=[
            vmem((2, firsts, seconds, cols), BF16),
            vmem((2, group, firsts * PAIR, cols), BF16),
            vmem((chunks, rows, CORES * cols), BF16),
            vmem((rows, CORES * cols), BF16),
            vmem((rows, CORES * cols), BF16),
            vmem((firsts, TILE), F32),
            vmem((occ_all, CORES * TILE), F32),
            vmem((depth, CORES * cols, width), BF16),
            vmem((chunks, depth, rows, width), BF16),
            vmem((chunks, depth + 1, rows, width), BF16),
            vmem((rows, width), F32),
            vmem((chunks, rows, width), BF16),
            vmem((chunks, group, firsts * PAIR, half), BF16),
            vmem((firsts, occ_all, half), BF16),
            vmem((count, count), BF16),
            vmem((count, count), BF16),
            vmem((rows, rows), BF16),
            dma((2,)),
            dma((2,)),
            dma((chunks, group)),
            dma((chunks, group)),
            dma((group,)),
            dma((group,)),
            dma((depth,)),
            dma(()),
            dma(()),
            dma((chunks, depth)),
            dma((chunks, depth)),
            dma((chunks, depth)),
            dma((chunks,)),
            dma((chunks, group)),
            dma((chunks, group)),
            dma((chunks,)),
        ],
        compiler_params=pltpu.CompilerParams(
            collective_id=0, has_side_effects=True, vmem_limit_bytes=58 * 1024 * 1024
        ),
        name="residual",
    )(
        amplitudes.reshape(firsts, occ_all, cols),
        amp_tiles,
        occ_coupling,
        integrals,
        int_tiles,
    )
    step = min(4, firsts)
    return pl.pallas_call(
        transpose_kernel,
        grid=(firsts // step,),
        in_specs=[pl.BlockSpec((step, occ_all, half), lambda g: (g, 0, 0))],
        out_specs=pl.BlockSpec((half, step * occ_all), lambda g: (0, g)),
        out_shape=jax.ShapeDtypeStruct((half, local_rows), BF16),
        name="turn",
    )(gathered)


def solution(mesh):
    shape = mesh.devices.shape
    in_specs = (P("bulk", "cuts"), P("bulk", "cuts"), P(), P("cuts", None), P("cuts", None))
    return jax.shard_map(
        functools.partial(shards, shape),
        mesh=mesh,
        in_specs=in_specs,
        out_specs=P("cuts", "bulk"),
        check_vma=False,
    )
```

```python
import functools

import jax
import jax.numpy as jnp
from jax import lax
from jax.experimental import pallas as pl
from jax.experimental.pallas import tpu as pltpu
from jax.sharding import PartitionSpec as P

TILE = 128
CORES = 2
LEAST = 16
BLOCK = 256
MESH = pl.DeviceIdType.MESH
F32 = jnp.float32
BF16 = jnp.bfloat16


def dot(a, b):
    return jnp.dot(a, b, preferred_element_type=F32)


def iota(shape, axis):
    return lax.broadcasted_iota(jnp.int32, shape, axis)


def one_hot(condition):
    return jnp.where(condition, 1.0, 0.0).astype(BF16)


class Sizes:
    def __init__(self, mesh_shape, amplitudes, occ_coupling, integrals):
        self.bulk, cuts = mesh_shape
        self.depth = cuts // CORES
        self.group = self.bulk * CORES
        local_rows, self.cols = amplitudes.shape
        self.occ = occ_coupling.shape[0]
        self.firsts = local_rows // self.occ
        self.pair = max(1, LEAST // self.firsts)
        self.seconds = self.pair * self.group
        self.chunks = self.occ // self.seconds
        self.load = max(LEAST, self.seconds)
        self.per_load = self.load // self.seconds
        self.loads = self.occ // self.load
        self.width = integrals.shape[1] // self.depth
        self.half = self.width // CORES
        self.rows = self.pair * self.occ
        self.block = self.firsts * self.pair
        self.sub_j = min(self.load, max(LEAST, BLOCK // self.firsts))
        self.sub_i = min(self.firsts, BLOCK // self.sub_j)
        self.count = self.sub_i * self.sub_j
        self.tiles = self.width // TILE
        self.flat = self.tiles * self.rows
        self.sent = (self.depth - 1) * self.flat
        self.can_pack = self.pair == 1 and self.depth == 4 and self.occ == TILE
        self.room = self.sent * 26 // 32 // LEAST * LEAST


def residual_kernel(s, pack, *refs):
    (
        amp_hbm,
        tiles_hbm,
        occ_ref,
        int_hbm,
        int_tiles_hbm,
        out_hbm,
        flag_ref,
        x_buf,
        send_buf,
        slab,
        tau,
        mask,
        tiles_ref,
        int_tiles_ref,
        map_send,
        map_recv,
        ints,
        part,
        inbox,
        acc,
        c_send,
        c_recv,
        turned,
        split_rows,
        mix,
        x_sem,
        tiles_sem,
        a_send_sem,
        a_recv_sem,
        map_send_sem,
        map_recv_sem,
        int_local_sem,
        int_send_sem,
        int_recv_sem,
        z_send_sem,
        right_sem,
        left_sem,
        c_send_sem,
        c_recv_sem,
        out_sem,
    ) = refs[:40]
    if pack:
        (
            choose,
            packed,
            spots,
            right_spots,
            left_spots,
            int_map,
            spot_send_sem,
            right_spot_sem,
            left_spot_sem,
            int_map_send_sem,
            int_map_recv_sem,
        ) = refs[40:]
    depth, group, chunks, cols, pair = s.depth, s.group, s.chunks, s.cols, s.pair
    block, half, flat = s.block, s.half, s.flat
    b = lax.axis_index("bulk")
    cut = lax.axis_index("cuts")
    z = cut // CORES
    core = cut % CORES
    me = b * CORES + core
    last = depth - 1

    def aligned(start, size):
        return pl.ds(pl.multiple_of(start, size), size)

    def at_rank(rank):
        return (rank // CORES, z * CORES + rank % CORES)

    def along(zz):
        return (b, zz * CORES + core)

    def remote(src, dst, send_sem, recv_sem, device):
        return pltpu.make_async_remote_copy(
            src_ref=src,
            dst_ref=dst,
            send_sem=send_sem,
            recv_sem=recv_sem,
            device_id=device,
            device_id_type=MESH,
        )

    def each_peer(body):
        def step(k, carry):
            body((me + k) % group)
            return carry

        lax.fori_loop(1, group, step, 0)

    def x_copy(u):
        return pltpu.make_async_copy(
            amp_hbm.at[:, aligned(u * s.load, s.load), :], x_buf.at[u % 2], x_sem.at[u % 2]
        )

    def place(n, rank):
        return slab.at[n, aligned((rank // CORES) * block, block), aligned((rank % CORES) * cols, cols)]

    def outgoing(n, to):
        return send_buf.at[(n // s.per_load) % 2, (n % s.per_load) * group + to]

    def a_copy(n, to):
        return remote(
            outgoing(n, to), place(n, me), a_send_sem.at[n], a_recv_sem.at[n], at_rank(to)
        )

    def a_arrived(n):
        return pltpu.make_async_copy(slab.at[n], slab.at[n], a_recv_sem.at[n])

    def a_left(n):
        ref = send_buf.at[(n // s.per_load) % 2, pl.ds((n % s.per_load) * group, group - 1)]
        return pltpu.make_async_copy(ref, ref, a_send_sem.at[n])

    def map_place(source):
        return map_recv.at[
            aligned((source // CORES) * s.firsts, s.firsts), aligned((source % CORES) * TILE, TILE)
        ]

    def map_copy(to, source):
        return remote(
            map_send, map_place(source), map_send_sem.at[to], map_recv_sem.at[source], at_rank(to)
        )

    def int_local(d):
        return pltpu.make_async_copy(
            int_hbm.at[:, pl.ds(d * s.width, s.width)],
            ints.at[d, aligned(core * cols, cols), :],
            int_local_sem.at[d],
        )

    def int_copy(source):
        return remote(
            ints.at[:, aligned(core * cols, cols), :],
            ints.at[:, aligned(source * cols, cols), :],
            int_send_sem,
            int_recv_sem,
            at_rank(b * CORES + 1 - core),
        )

    def right_copy(n, d):
        return remote(
            part.at[n, d],
            inbox.at[n, d + 1],
            z_send_sem.at[n, d],
            right_sem.at[n, d],
            along((z + 1) % depth),
        )

    def left_copy(n, d):
        return remote(
            part.at[n, d],
            inbox.at[n, d],
            z_send_sem.at[n, d],
            left_sem.at[n, d],
            along((z + last) % depth),
        )

    def c_copy(n, to):
        return remote(
            c_send.at[n, aligned((to // CORES) * block, block), aligned((to % CORES) * half, half)],
            c_recv.at[n, me],
            c_send_sem.at[n],
            c_recv_sem.at[n],
            at_rank(to),
        )

    def c_own(n):
        return pltpu.make_async_copy(
            c_send.at[n, aligned(b * block, block), aligned(core * half, half)],
            c_recv.at[n, me],
            c_recv_sem.at[n],
        )

    def c_arrived(n):
        return pltpu.make_async_copy(c_recv.at[n], c_recv.at[n], c_recv_sem.at[n])

    def c_left(n):
        ref = c_recv.at[n, pl.ds(0, group - 1)]
        return pltpu.make_async_copy(ref, ref, c_send_sem.at[n])

    def prepare(u):
        x_copy(u).wait()
        for gi in range(s.firsts // s.sub_i):
            for gj in range(s.load // s.sub_j):
                x = x_buf[
                    u % 2,
                    gi * s.sub_i : (gi + 1) * s.sub_i,
                    gj * s.sub_j : (gj + 1) * s.sub_j,
                    :,
                ]
                y = dot(split_rows[...], x.reshape(s.count, cols)).astype(BF16)
                send_buf[
                    u % 2,
                    gj * s.sub_j // pair : (gj + 1) * s.sub_j // pair,
                    gi * s.sub_i * pair : (gi + 1) * s.sub_i * pair,
                    :,
                ] = y.reshape(s.sub_j // pair, s.sub_i * pair, cols)
        pl.when(u + 2 < s.loads)(lambda: x_copy(u + 2).start())

    def send_amplitudes(n):
        each_peer(lambda to: a_copy(n, to).start())
        pltpu.make_async_copy(outgoing(n, me), place(n, me), a_recv_sem.at[n]).start()

    def dress(n):
        span = min(512, CORES * cols)
        for at in range(0, CORES * cols, span):
            kept = mask[:, at : at + span]
            masked = slab[n, :, at : at + span] * kept
            mixed = dot(mix[...], masked)
            dressed = (masked.astype(F32) + mixed).astype(BF16)
            tau[:, at : at + span] = dressed * kept

    tiles_copy = pltpu.make_async_copy(tiles_hbm, tiles_ref, tiles_sem.at[0])
    int_tiles_copy = pltpu.make_async_copy(int_tiles_hbm, int_tiles_ref, tiles_sem.at[1])
    x_copy(0).start()
    tiles_copy.start()
    int_tiles_copy.start()
    barrier = pltpu.get_barrier_semaphore()

    def greet(device):
        pl.semaphore_signal(barrier, inc=1, device_id=device, device_id_type=MESH)

    each_peer(lambda to: greet(at_rank(to)))
    pl.when(z > 0)(lambda: greet(along(z - 1)))
    pl.when(z < last)(lambda: greet(along(z + 1)))
    for d in range(depth):
        int_local(d).start()
    if s.loads > 1:
        x_copy(1).start()

    r, c = iota((s.count, s.count), 0), iota((s.count, s.count), 1)
    natural = ((r // pair) % s.sub_i) * s.sub_j + (r // (pair * s.sub_i)) * pair + r % pair
    split_rows[...] = one_hot(c == natural)
    prepare(0)
    for u in range(1, 1 // s.per_load + 1):
        if u < s.loads:
            prepare(u)
    tiles_copy.wait()
    int_tiles_copy.wait()
    kept_tiles = tiles_ref[...].astype(F32)
    map_send[...] = jnp.concatenate(
        [kept_tiles, jnp.zeros((s.firsts, TILE - kept_tiles.shape[1]), F32)], axis=1
    )
    own_tiles = cols // TILE
    if pack:
        int_tiles = int_tiles_ref[...].astype(F32)
        int_map[aligned(core * own_tiles, own_tiles), :] = jnp.concatenate(
            [int_tiles, jnp.zeros((own_tiles, TILE - int_tiles.shape[1]), F32)], axis=1
        )

    ends = jnp.where(z > 0, 1, 0) + jnp.where(z < last, 1, 0)
    pl.semaphore_wait(barrier, group - 1 + ends)

    each_peer(lambda to: map_copy(to, me).start())
    own_map = pltpu.make_async_copy(map_send, map_place(me), map_recv_sem.at[me])
    own_map.start()
    if pack:

        def int_map_copy(source):
            span = aligned(source * own_tiles, own_tiles)
            mine = aligned(core * own_tiles, own_tiles)
            return remote(
                int_map.at[mine],
                int_map.at[span],
                int_map_send_sem,
                int_map_recv_sem,
                at_rank(b * CORES + 1 - core),
            )

        int_map_copy(core).start()
    send_amplitudes(0)

    for d in range(depth):
        int_local(d).wait()
        int_tiles = int_tiles_ref[:, d * s.tiles : (d + 1) * s.tiles].astype(BF16)
        spread = one_hot(iota((s.tiles, s.width), 1) // TILE == iota((s.tiles, s.width), 0))
        kept = dot(int_tiles, spread).astype(BF16)
        for k in range(own_tiles):
            span = aligned(core * cols + k * TILE, TILE)
            ints[d, span, :] = ints[d, span, :] * kept[k : k + 1, :]
    int_copy(core).start()

    tall = one_hot(iota((s.rows, s.occ), 0) // pair == iota((s.rows, s.occ), 1))
    if pair == 1:
        mix[...] = occ_ref[...]
    else:
        wide = one_hot(iota((s.occ, s.rows), 1) // pair == iota((s.occ, s.rows), 0))
        stretched = dot(dot(tall, occ_ref[...]).astype(BF16), wide)
        same = iota((s.rows, s.rows), 0) % pair == iota((s.rows, s.rows), 1) % pair
        mix[...] = jnp.where(same, stretched, 0.0).astype(BF16)

    own_map.wait()
    each_peer(lambda source: map_copy(source, source).wait_recv())
    tiles_all = dot(tall, map_recv[...].astype(BF16)).astype(BF16)
    lane = iota((CORES * TILE, CORES * cols), 0)
    col = iota((CORES * TILE, CORES * cols), 1)
    mask[...] = dot(
        tiles_all, one_hot(lane == (col // cols) * TILE + (col % cols) // TILE)
    ).astype(BF16)

    if pack:
        others = (depth - 1) * s.tiles
        room = s.room

        def spot_copy(src, sem, dst, recv, device):
            return remote(src, dst, sem, recv, device)

        def right_spot(src):
            return remote(
                src, right_spots, spot_send_sem.at[0], right_spot_sem, along((z + 1) % depth)
            )

        def left_spot(src):
            return remote(
                src, left_spots, spot_send_sem.at[1], left_spot_sem, along((z + last) % depth)
            )

        int_map_copy(1 - core).wait_recv()

        @pl.when((z == 0) | (z == last))
        def _():
            hits = jnp.zeros((s.occ, TILE), F32)
            for k in range(CORES):
                rows = int_map[k * own_tiles : (k + 1) * own_tiles, :]
                rows = jnp.concatenate([rows, jnp.zeros((TILE - own_tiles, TILE), F32)], axis=0)
                hits += dot(
                    map_recv[:, k * TILE : (k + 1) * TILE].astype(BF16), rows.astype(BF16)
                )
            hits = jnp.where(hits > 0.5, 1.0, 0.0).T
            hits = jnp.where(z == 0, hits[s.tiles : s.tiles + others], hits[:others])
            hits = jnp.concatenate([hits, jnp.zeros((LEAST - others, TILE), F32)], axis=0)
            marks = hits.astype(BF16)
            i, k = iota((TILE, TILE), 0), iota((TILE, TILE), 1)
            ahead = dot(marks, one_hot(i < k))
            totals = dot(marks, jnp.ones((TILE, TILE), BF16))
            r, c = iota((LEAST, LEAST), 0), iota((LEAST, LEAST), 1)
            before = jnp.where(z == 0, one_hot(c > r), one_hot(c < r))
            ahead += dot(before, totals.astype(BF16))
            spots[0:LEAST, :] = jnp.where(hits > 0.5, ahead, -1.0)
            total = jnp.sum(hits, axis=0, keepdims=True)
            total = jnp.sum(total, axis=1, keepdims=True)
            spots[LEAST:, :] = jnp.broadcast_to(total, (spots.shape[0] - LEAST, TILE))
            pl.when(z == 0)(lambda: right_spot(spots).start())
            pl.when(z == last)(lambda: left_spot(spots).start())
            at = iota((room, TILE), 0).astype(F32)
            for k in range(others):
                choose[0:room, k * TILE : (k + 1) * TILE] = one_hot(at == spots[k : k + 1, :])

        def restore(ref):
            where = jnp.concatenate(
                [ref[0:LEAST, :], jnp.full((TILE - LEAST, TILE), -1.0, F32)], axis=0
            ).T
            at = iota((TILE, room), 1).astype(F32)
            for k in range(others):
                choose[k * TILE : (k + 1) * TILE, 0:room] = one_hot(at == where[:, k : k + 1])

        @pl.when(z == 1)
        def _():
            right_spot(spots).wait_recv()
            right_spot(right_spots).start()
            restore(right_spots)

        @pl.when(z == last - 1)
        def _():
            left_spot(spots).wait_recv()
            left_spot(left_spots).start()
            restore(left_spots)

        pieces = []
        for o in range(depth - 1):
            if o * flat < room:
                pieces.append((o * flat, min(room, (o + 1) * flat)))

        def packed_copy(n, o, to_right):
            begin, end = pieces[o]
            base = 2 * flat if to_right else 0
            return remote(
                packed.at[n % 2, pl.ds(begin, end - begin), :],
                inbox_rows(n, base + begin, end - begin),
                z_send_sem.at[n, o],
                (right_sem if to_right else left_sem).at[n, o],
                along((z + 1) % depth) if to_right else along((z + last) % depth),
            )

        def inbox_rows(n, begin, size):
            slot = begin // flat
            return inbox.at[n, slot, pl.ds(begin - slot * flat, size), :]

        def packed_left(n):
            for o in range(len(pieces)):
                packed_copy(n, o, True).wait_send()

    for at in range(0, turned.shape[1], 512):
        turned[:, at : at + 512] = jnp.zeros((half, 512), BF16)
    int_copy(1 - core).wait_recv()

    farther = jnp.maximum(z, last - z)
    dense_right = (z > 0) if not pack else (z > 1)
    dense_left = (z < last) if not pack else (z < last - 1)

    def add_into(n, d, slot):
        part[n, d] = (part[n, d].astype(F32) + inbox[n, slot].astype(F32)).astype(BF16)

    def ladder_step(t):
        a_arrived(t).wait()
        pl.when(t + 1 < chunks)(lambda: send_amplitudes(t + 1))
        dress(t)

        def ladder(k, carry):
            d = jnp.where(z * 2 < depth, last - k, k)
            y = dot(tau[...], ints[d]).astype(BF16)
            for k in range(s.tiles):
                part[t, d, k * s.rows : (k + 1) * s.rows, :] = y[:, k * TILE : (k + 1) * TILE]
            if not pack:
                pl.when((z == 0) & (d > 0))(lambda: right_copy(t, d).start())
                pl.when((z == last) & (d < last))(lambda: left_copy(t, d).start())
            return carry

        lax.fori_loop(0, depth, ladder, 0)
        if pack:

            @pl.when((z == 0) | (z == last))
            def _():
                pl.when(t >= 2)(lambda: packed_left(t - 2))
                first = jnp.where(z == 0, 1, 0)
                x = part[t, pl.ds(first, depth - 1)].reshape(s.sent, TILE)
                for o, (begin, end) in enumerate(pieces):
                    packed[t % 2, begin:end, :] = dot(choose[begin:end, :], x).astype(BF16)
                    pl.when(z == 0)(lambda: packed_copy(t, o, True).start())
                    pl.when(z == last)(lambda: packed_copy(t, o, False).start())

        a_left(t).wait()
        ready = t + 2
        pl.when((ready < chunks) & (ready % s.per_load == 0))(
            lambda: prepare(ready // s.per_load)
        )

    def unpack_step(m, to_right):
        base = 2 if to_right else 0
        for o in range(depth - 1):
            if o < len(pieces):
                packed_copy(m, o, to_right).wait_recv()
            end = pieces[min(o, len(pieces) - 1)][1]
            x = inbox[m, base : base + depth - 1].reshape(s.sent, TILE)[:end]
            k = depth - 2 - o if to_right else o
            d = k + 1 if to_right else k
            y = dot(choose[k * flat : (k + 1) * flat, :end], x)
            part[m, d] = (part[m, d].astype(F32) + y).astype(BF16)
            if to_right and d > 1:
                right_copy(m, d).start()
            if not to_right and d < depth - 2:
                left_copy(m, d).start()

    def right_step(m):
        def pass_on(k, carry):
            d = last - k
            right_copy(m, d).wait_recv()
            add_into(m, d, d + 1)
            right_copy(m, d).start()
            return carry

        lax.fori_loop(0, last - z, pass_on, 0)

    def left_step(m):
        def pass_on(d, carry):
            left_copy(m, d).wait_recv()
            add_into(m, d, d)
            left_copy(m, d).start()
            return carry

        lax.fori_loop(0, z, pass_on, 0)

    def last_step(m):
        acc[...] = part[m, z].astype(F32)

        @pl.when(dense_right)
        def _():
            right_copy(m, z).wait_recv()
            acc[...] += inbox[m, z + 1].astype(F32)

        @pl.when(dense_left)
        def _():
            left_copy(m, z).wait_recv()
            acc[...] += inbox[m, z].astype(F32)

        for k in range(s.tiles):
            c_send[m, :, k * TILE : (k + 1) * TILE] = acc[k * s.rows : (k + 1) * s.rows, :].astype(
                BF16
            )
        each_peer(lambda to: c_copy(m, to).start())
        c_own(m).start()

    def turn_step(u):
        for k in range(s.per_load):
            c_arrived(u * s.per_load + k).wait()
        span = s.sub_i * s.occ
        r = iota((s.count, 1), 0)
        spot = ((r // pair) % s.sub_i) * s.occ + (r // (pair * s.sub_i)) * pair + r % pair
        per = s.sub_j // pair
        for gj in range(s.load // s.sub_j):
            place_j = one_hot(iota((s.count, span), 1) - (u * s.load + gj * s.sub_j) == spot)
            for gi in range(s.firsts // s.sub_i):
                pieces = []
                begin = gj * per
                while begin < (gj + 1) * per:
                    end = min((gj + 1) * per, (begin // group + 1) * group)
                    k = begin // group
                    pieces.append(
                        c_recv[
                            u * s.per_load + k,
                            begin - k * group : end - k * group,
                            gi * s.sub_i * pair : (gi + 1) * s.sub_i * pair,
                            :,
                        ]
                    )
                    begin = end
                x = jnp.concatenate(pieces, axis=0) if len(pieces) > 1 else pieces[0]
                x = x.reshape(s.count, half).T
                step = min(512, span)
                for at in range(0, span, step):
                    y = dot(x, place_j[:, at : at + step]).astype(BF16)
                    cols_at = gi * span + at
                    turned[:, cols_at : cols_at + step] = turned[:, cols_at : cols_at + step] + y

    def step(t, carry):
        pl.when(t < chunks)(lambda: ladder_step(t))

        m = t - z
        live = (m >= 0) & (m < chunks)
        if pack:
            pl.when((z == 1) & live)(lambda: unpack_step(m, True))
        pl.when(dense_right & live)(lambda: right_step(m))

        m_left = t - (last - z)
        live_left = (m_left >= 0) & (m_left < chunks)
        if pack:
            pl.when((z == last - 1) & live_left)(lambda: unpack_step(m_left, False))
        pl.when(dense_left & live_left)(lambda: left_step(m_left))

        m_last = t - farther
        pl.when((m_last >= 0) & (m_last < chunks))(lambda: last_step(m_last))

        m_out = t - farther - 1
        whole = m_out % s.per_load == s.per_load - 1
        pl.when((m_out >= 0) & (m_out < chunks) & whole)(lambda: turn_step(m_out // s.per_load))

        return carry

    lax.fori_loop(0, chunks + depth, step, 0)

    out_copy = pltpu.make_async_copy(turned, out_hbm, out_sem)
    out_copy.start()
    if pack:

        @pl.when(z > 1)
        def _():
            right_spot(spots).wait_recv()
            pl.when(z < last)(lambda: right_spot(right_spots).start())

        @pl.when(z < last - 1)
        def _():
            left_spot(spots).wait_recv()
            pl.when(z > 0)(lambda: left_spot(left_spots).start())

        pl.when(z < last)(lambda: right_spot(spots).wait_send())
        pl.when(z > 0)(lambda: left_spot(spots).wait_send())
        rows = slice(LEAST, LEAST + 8)
        from_left = jnp.where(z == 0, spots[rows, :], right_spots[rows, :])
        from_right = jnp.where(z == last, spots[rows, :], left_spots[rows, :])
        flag_ref[...] = jnp.maximum(from_left, from_right)
        int_map_copy(core).wait_send()

        @pl.when((z == 0) | (z == last))
        def _():
            for n in range(max(0, chunks - 2), chunks):
                packed_left(n)

    else:
        flag_ref[...] = jnp.zeros(flag_ref.shape, F32)

    each_peer(lambda to: map_copy(to, me).wait_send())
    int_copy(core).wait_send()
    dense_sender = jnp.where((z > 0) & (z < last), True, not pack)

    def finish(n, carry):
        def sent(d, carry):
            pl.when((d != z) & dense_sender)(lambda: right_copy(n, d).wait_send())
            return carry

        lax.fori_loop(0, depth, sent, 0)
        c_left(n).wait()
        return carry

    lax.fori_loop(0, chunks, finish, 0)
    out_copy.wait()


def residual(s, pack, amplitudes, amp_tiles, occ_coupling, integrals, int_tiles):
    vmem, dma = pltpu.VMEM, pltpu.SemaphoreType.DMA
    any_space = pl.BlockSpec(memory_space=pl.ANY)
    in_vmem = pl.BlockSpec(memory_space=pltpu.VMEM)
    chunks, depth, group = s.chunks, s.depth, s.group
    both = CORES * s.cols
    scratch = [
        vmem((2, s.firsts, s.load, s.cols), BF16),
        vmem((2, s.per_load * group, s.block, s.cols), BF16),
        vmem((chunks, s.rows, both), BF16),
        vmem((s.rows, both), BF16),
        vmem((s.rows, both), BF16),
        vmem(amp_tiles.shape, jnp.int32),
        vmem(int_tiles.shape, jnp.int32),
        vmem((s.firsts, TILE), F32),
        vmem((s.occ, CORES * TILE), F32),
        vmem((depth, both, s.width), BF16),
        vmem((chunks, depth, s.flat, TILE), BF16),
        vmem((chunks, depth + 1, s.flat, TILE), BF16),
        vmem((s.flat, TILE), F32),
        vmem((chunks, s.rows, s.width), BF16),
        vmem((chunks, group, s.block, s.half), BF16),
        vmem((s.half, s.firsts * s.occ), BF16),
        vmem((s.count, s.count), BF16),
        vmem((s.rows, s.rows), BF16),
        dma((2,)),
        dma((2,)),
        dma((chunks,)),
        dma((chunks,)),
        dma((group,)),
        dma((group,)),
        dma((depth,)),
        dma(()),
        dma(()),
        dma((chunks, depth)),
        dma((chunks, depth)),
        dma((chunks, depth)),
        dma((chunks,)),
        dma((chunks,)),
        dma(()),
    ]
    if pack:
        scratch += [
            vmem((s.sent, s.sent), BF16),
            vmem((2, s.room, TILE), BF16),
            vmem((LEAST + 8, TILE), F32),
            vmem((LEAST + 8, TILE), F32),
            vmem((LEAST + 8, TILE), F32),
            vmem((CORES * (s.cols // TILE), TILE), F32),
            dma((2,)),
            dma(()),
            dma(()),
            dma(()),
            dma(()),
        ]
    return pl.pallas_call(
        functools.partial(residual_kernel, s, pack),
        out_shape=(
            jax.ShapeDtypeStruct((s.half, s.firsts * s.occ), BF16),
            jax.ShapeDtypeStruct((8, TILE), F32),
        ),
        in_specs=[any_space, any_space, in_vmem, any_space, any_space],
        out_specs=(any_space, in_vmem),
        scratch_shapes=scratch,
        compiler_params=pltpu.CompilerParams(
            collective_id=1 if pack else 0,
            has_side_effects=True,
            vmem_limit_bytes=58 * 1024 * 1024,
        ),
        name="packed" if pack else "dense",
    )(
        amplitudes.reshape(s.firsts, s.occ, s.cols),
        amp_tiles,
        occ_coupling,
        integrals,
        int_tiles,
    )


def shards(mesh_shape, *arrays):
    s = Sizes(mesh_shape, arrays[0], arrays[2], arrays[3])
    if PACK and s.can_pack:
        out, used = residual(s, True, *arrays)
        return lax.cond(
            used[0, 0] > s.room, lambda: residual(s, False, *arrays)[0], lambda: out
        )
    return residual(s, False, *arrays)[0]


PACK = False


def solution(mesh):
    shape = mesh.devices.shape
    in_specs = (P("bulk", "cuts"), P("bulk", "cuts"), P(), P("cuts", None), P("cuts", None))
    return jax.shard_map(
        functools.partial(shards, shape),
        mesh=mesh,
        in_specs=in_specs,
        out_specs=P("cuts", "bulk"),
        check_vma=False,
    )
```

```python
import functools

import jax
import jax.numpy as jnp
from jax import lax
from jax.experimental import pallas as pl
from jax.experimental.pallas import tpu as pltpu
from jax.sharding import PartitionSpec as P

TILE = 128
CORES = 2
LEAST = 16
BLOCK = 256
AHEAD = 2
MESH = pl.DeviceIdType.MESH
F32 = jnp.float32
BF16 = jnp.bfloat16


def dot(a, b):
    return jnp.dot(a, b, preferred_element_type=F32)


def iota(shape, axis):
    return lax.broadcasted_iota(jnp.int32, shape, axis)


def one_hot(condition):
    return jnp.where(condition, 1.0, 0.0).astype(BF16)


class Sizes:
    def __init__(self, mesh_shape, amplitudes, occ_coupling, integrals):
        self.bulk, cuts = mesh_shape
        self.depth = cuts // CORES
        self.group = self.bulk * CORES
        local_rows, self.cols = amplitudes.shape
        self.occ = occ_coupling.shape[0]
        self.firsts = local_rows // self.occ
        self.pair = max(1, LEAST // self.firsts)
        self.seconds = self.pair * self.group
        self.chunks = self.occ // self.seconds
        self.load = max(LEAST, self.seconds)
        self.per_load = self.load // self.seconds
        self.loads = self.occ // self.load
        self.slots = 2 if self.per_load > 1 else AHEAD + 2
        self.width = integrals.shape[1] // self.depth
        self.half = self.width // CORES
        self.rows = self.pair * self.occ
        self.block = self.firsts * self.pair
        self.sub_j = min(self.load, max(LEAST, BLOCK // self.firsts))
        self.sub_i = min(self.firsts, BLOCK // self.sub_j)
        self.count = self.sub_i * self.sub_j
        self.tiles = self.width // TILE
        self.flat = self.tiles * self.rows
        self.sent = (self.depth - 1) * self.flat
        self.can_pack = self.pair == 1 and self.depth == 4 and self.occ == TILE
        self.room = self.sent * 26 // 32 // LEAST * LEAST


def residual_kernel(s, pack, *refs):
    (
        amp_hbm,
        tiles_hbm,
        occ_ref,
        int_hbm,
        int_tiles_hbm,
        out_hbm,
        flag_ref,
        x_buf,
        send_buf,
        slab,
        tau,
        mask,
        tiles_ref,
        int_tiles_ref,
        map_send,
        map_recv,
        ints,
        part,
        inbox,
        acc,
        c_send,
        c_recv,
        turned,
        split_rows,
        mix,
        x_sem,
        tiles_sem,
        a_send_sem,
        a_recv_sem,
        map_send_sem,
        map_recv_sem,
        int_local_sem,
        int_send_sem,
        int_recv_sem,
        z_send_sem,
        right_sem,
        left_sem,
        c_send_sem,
        c_recv_sem,
        out_sem,
    ) = refs[:40]
    if pack:
        (
            choose,
            packed,
            spots,
            right_spots,
            left_spots,
            int_map,
            spot_send_sem,
            right_spot_sem,
            left_spot_sem,
            int_map_send_sem,
            int_map_recv_sem,
        ) = refs[40:]
    depth, group, chunks, cols, pair = s.depth, s.group, s.chunks, s.cols, s.pair
    block, half, flat = s.block, s.half, s.flat
    b = lax.axis_index("bulk")
    cut = lax.axis_index("cuts")
    z = cut // CORES
    core = cut % CORES
    me = b * CORES + core
    last = depth - 1

    def aligned(start, size):
        return pl.ds(pl.multiple_of(start, size), size)

    def at_rank(rank):
        return (rank // CORES, z * CORES + rank % CORES)

    def along(zz):
        return (b, zz * CORES + core)

    def remote(src, dst, send_sem, recv_sem, device):
        return pltpu.make_async_remote_copy(
            src_ref=src,
            dst_ref=dst,
            send_sem=send_sem,
            recv_sem=recv_sem,
            device_id=device,
            device_id_type=MESH,
        )

    def each_peer(body):
        def step(k, carry):
            body((me + k) % group)
            return carry

        lax.fori_loop(1, group, step, 0)

    def x_copy(u):
        return pltpu.make_async_copy(
            amp_hbm.at[:, aligned(u * s.load, s.load), :], x_buf.at[u % 2], x_sem.at[u % 2]
        )

    def place(n, rank):
        return slab.at[n, aligned((rank // CORES) * block, block), aligned((rank % CORES) * cols, cols)]

    def outgoing(n, to):
        return send_buf.at[(n // s.per_load) % s.slots, (n % s.per_load) * group + to]

    def a_copy(n, to):
        return remote(
            outgoing(n, to), place(n, me), a_send_sem.at[n], a_recv_sem.at[n], at_rank(to)
        )

    def a_arrived(n):
        return pltpu.make_async_copy(slab.at[n], slab.at[n], a_recv_sem.at[n])

    def a_left(n):
        ref = send_buf.at[(n // s.per_load) % s.slots, pl.ds((n % s.per_load) * group, group - 1)]
        return pltpu.make_async_copy(ref, ref, a_send_sem.at[n])

    def map_place(source):
        return map_recv.at[
            aligned((source // CORES) * s.firsts, s.firsts), aligned((source % CORES) * TILE, TILE)
        ]

    def map_copy(to, source):
        return remote(
            map_send, map_place(source), map_send_sem.at[to], map_recv_sem.at[source], at_rank(to)
        )

    def int_local(d):
        return pltpu.make_async_copy(
            int_hbm.at[:, pl.ds(d * s.width, s.width)],
            ints.at[d, aligned(core * cols, cols), :],
            int_local_sem.at[d],
        )

    def int_copy(source):
        return remote(
            ints.at[:, aligned(core * cols, cols), :],
            ints.at[:, aligned(source * cols, cols), :],
            int_send_sem,
            int_recv_sem,
            at_rank(b * CORES + 1 - core),
        )

    def right_copy(n, d):
        return remote(
            part.at[n, d],
            inbox.at[n, d + 1],
            z_send_sem.at[n, d],
            right_sem.at[n, d],
            along((z + 1) % depth),
        )

    def left_copy(n, d):
        return remote(
            part.at[n, d],
            inbox.at[n, d],
            z_send_sem.at[n, d],
            left_sem.at[n, d],
            along((z + last) % depth),
        )

    def c_copy(n, to):
        return remote(
            c_send.at[n, aligned((to // CORES) * block, block), aligned((to % CORES) * half, half)],
            c_recv.at[n, me],
            c_send_sem.at[n],
            c_recv_sem.at[n],
            at_rank(to),
        )

    def c_own(n):
        return pltpu.make_async_copy(
            c_send.at[n, aligned(b * block, block), aligned(core * half, half)],
            c_recv.at[n, me],
            c_recv_sem.at[n],
        )

    def c_arrived(n):
        return pltpu.make_async_copy(c_recv.at[n], c_recv.at[n], c_recv_sem.at[n])

    def c_left(n):
        ref = c_recv.at[n, pl.ds(0, group - 1)]
        return pltpu.make_async_copy(ref, ref, c_send_sem.at[n])

    def prepare(u):
        x_copy(u).wait()
        for gi in range(s.firsts // s.sub_i):
            for gj in range(s.load // s.sub_j):
                x = x_buf[
                    u % 2,
                    gi * s.sub_i : (gi + 1) * s.sub_i,
                    gj * s.sub_j : (gj + 1) * s.sub_j,
                    :,
                ]
                y = dot(split_rows[...], x.reshape(s.count, cols)).astype(BF16)
                send_buf[
                    u % s.slots,
                    gj * s.sub_j // pair : (gj + 1) * s.sub_j // pair,
                    gi * s.sub_i * pair : (gi + 1) * s.sub_i * pair,
                    :,
                ] = y.reshape(s.sub_j // pair, s.sub_i * pair, cols)
        pl.when(u + 2 < s.loads)(lambda: x_copy(u + 2).start())

    def send_amplitudes(n):
        each_peer(lambda to: a_copy(n, to).start())
        pltpu.make_async_copy(outgoing(n, me), place(n, me), a_recv_sem.at[n]).start()

    def dress(n):
        span = min(512, CORES * cols)
        for at in range(0, CORES * cols, span):
            kept = mask[:, at : at + span]
            masked = slab[n, :, at : at + span] * kept
            mixed = dot(mix[...], masked)
            dressed = (masked.astype(F32) + mixed).astype(BF16)
            tau[:, at : at + span] = dressed * kept

    tiles_copy = pltpu.make_async_copy(tiles_hbm, tiles_ref, tiles_sem.at[0])
    int_tiles_copy = pltpu.make_async_copy(int_tiles_hbm, int_tiles_ref, tiles_sem.at[1])
    x_copy(0).start()
    tiles_copy.start()
    int_tiles_copy.start()
    barrier = pltpu.get_barrier_semaphore()

    def greet(device):
        pl.semaphore_signal(barrier, inc=1, device_id=device, device_id_type=MESH)

    each_peer(lambda to: greet(at_rank(to)))
    pl.when(z > 0)(lambda: greet(along(z - 1)))
    pl.when(z < last)(lambda: greet(along(z + 1)))
    for d in range(depth):
        int_local(d).start()
    if s.loads > 1:
        x_copy(1).start()

    r, c = iota((s.count, s.count), 0), iota((s.count, s.count), 1)
    natural = ((r // pair) % s.sub_i) * s.sub_j + (r // (pair * s.sub_i)) * pair + r % pair
    split_rows[...] = one_hot(c == natural)
    prepare(0)
    tiles_copy.wait()
    int_tiles_copy.wait()
    kept_tiles = tiles_ref[...].astype(F32)
    map_send[...] = jnp.concatenate(
        [kept_tiles, jnp.zeros((s.firsts, TILE - kept_tiles.shape[1]), F32)], axis=1
    )
    own_tiles = cols // TILE
    if pack:
        int_tiles = int_tiles_ref[...].astype(F32)
        int_map[aligned(core * own_tiles, own_tiles), :] = jnp.concatenate(
            [int_tiles, jnp.zeros((own_tiles, TILE - int_tiles.shape[1]), F32)], axis=1
        )

    ends = jnp.where(z > 0, 1, 0) + jnp.where(z < last, 1, 0)
    pl.semaphore_wait(barrier, group - 1 + ends)

    each_peer(lambda to: map_copy(to, me).start())
    own_map = pltpu.make_async_copy(map_send, map_place(me), map_recv_sem.at[me])
    own_map.start()
    if pack:

        def int_map_copy(source):
            span = aligned(source * own_tiles, own_tiles)
            mine = aligned(core * own_tiles, own_tiles)
            return remote(
                int_map.at[mine],
                int_map.at[span],
                int_map_send_sem,
                int_map_recv_sem,
                at_rank(b * CORES + 1 - core),
            )

        int_map_copy(core).start()
    send_amplitudes(0)

    for d in range(depth):
        int_local(d).wait()
        int_tiles = int_tiles_ref[:, d * s.tiles : (d + 1) * s.tiles].astype(BF16)
        spread = one_hot(iota((s.tiles, s.width), 1) // TILE == iota((s.tiles, s.width), 0))
        kept = dot(int_tiles, spread).astype(BF16)
        for k in range(own_tiles):
            span = aligned(core * cols + k * TILE, TILE)
            ints[d, span, :] = ints[d, span, :] * kept[k : k + 1, :]
    int_copy(core).start()
    for n in range(1, min(AHEAD, chunks)):
        if n % s.per_load == 0:
            prepare(n // s.per_load)
        send_amplitudes(n)
    if AHEAD < chunks and AHEAD % s.per_load == 0:
        prepare(AHEAD // s.per_load)

    tall = one_hot(iota((s.rows, s.occ), 0) // pair == iota((s.rows, s.occ), 1))
    if pair == 1:
        mix[...] = occ_ref[...]
    else:
        wide = one_hot(iota((s.occ, s.rows), 1) // pair == iota((s.occ, s.rows), 0))
        stretched = dot(dot(tall, occ_ref[...]).astype(BF16), wide)
        same = iota((s.rows, s.rows), 0) % pair == iota((s.rows, s.rows), 1) % pair
        mix[...] = jnp.where(same, stretched, 0.0).astype(BF16)

    own_map.wait()
    each_peer(lambda source: map_copy(source, source).wait_recv())
    tiles_all = dot(tall, map_recv[...].astype(BF16)).astype(BF16)
    lane = iota((CORES * TILE, CORES * cols), 0)
    col = iota((CORES * TILE, CORES * cols), 1)
    mask[...] = dot(
        tiles_all, one_hot(lane == (col // cols) * TILE + (col % cols) // TILE)
    ).astype(BF16)

    if pack:
        others = (depth - 1) * s.tiles
        room = s.room

        def spot_copy(src, sem, dst, recv, device):
            return remote(src, dst, sem, recv, device)

        def right_spot(src):
            return remote(
                src, right_spots, spot_send_sem.at[0], right_spot_sem, along((z + 1) % depth)
            )

        def left_spot(src):
            return remote(
                src, left_spots, spot_send_sem.at[1], left_spot_sem, along((z + last) % depth)
            )

        int_map_copy(1 - core).wait_recv()

        @pl.when((z == 0) | (z == last))
        def _():
            hits = jnp.zeros((s.occ, TILE), F32)
            for k in range(CORES):
                rows = int_map[k * own_tiles : (k + 1) * own_tiles, :]
                rows = jnp.concatenate([rows, jnp.zeros((TILE - own_tiles, TILE), F32)], axis=0)
                hits += dot(
                    map_recv[:, k * TILE : (k + 1) * TILE].astype(BF16), rows.astype(BF16)
                )
            hits = jnp.where(hits > 0.5, 1.0, 0.0).T
            hits = jnp.where(z == 0, hits[s.tiles : s.tiles + others], hits[:others])
            hits = jnp.concatenate([hits, jnp.zeros((LEAST - others, TILE), F32)], axis=0)
            marks = hits.astype(BF16)
            i, k = iota((TILE, TILE), 0), iota((TILE, TILE), 1)
            ahead = dot(marks, one_hot(i < k))
            totals = dot(marks, jnp.ones((TILE, TILE), BF16))
            r, c = iota((LEAST, LEAST), 0), iota((LEAST, LEAST), 1)
            before = jnp.where(z == 0, one_hot(c > r), one_hot(c < r))
            ahead += dot(before, totals.astype(BF16))
            spots[0:LEAST, :] = jnp.where(hits > 0.5, ahead, -1.0)
            total = jnp.sum(hits, axis=0, keepdims=True)
            total = jnp.sum(total, axis=1, keepdims=True)
            spots[LEAST:, :] = jnp.broadcast_to(total, (spots.shape[0] - LEAST, TILE))
            pl.when(z == 0)(lambda: right_spot(spots).start())
            pl.when(z == last)(lambda: left_spot(spots).start())
            at = iota((room, TILE), 0).astype(F32)
            for k in range(others):
                choose[0:room, k * TILE : (k + 1) * TILE] = one_hot(at == spots[k : k + 1, :])

        def restore(ref):
            where = jnp.concatenate(
                [ref[0:LEAST, :], jnp.full((TILE - LEAST, TILE), -1.0, F32)], axis=0
            ).T
            at = iota((TILE, room), 1).astype(F32)
            for k in range(others):
                choose[k * TILE : (k + 1) * TILE, 0:room] = one_hot(at == where[:, k : k + 1])

        @pl.when(z == 1)
        def _():
            right_spot(spots).wait_recv()
            right_spot(right_spots).start()
            restore(right_spots)

        @pl.when(z == last - 1)
        def _():
            left_spot(spots).wait_recv()
            left_spot(left_spots).start()
            restore(left_spots)

        pieces = []
        for o in range(depth - 1):
            if o * flat < room:
                pieces.append((o * flat, min(room, (o + 1) * flat)))

        def packed_copy(n, o, to_right):
            begin, end = pieces[o]
            base = 2 * flat if to_right else 0
            return remote(
                packed.at[n % 2, pl.ds(begin, end - begin), :],
                inbox_rows(n, base + begin, end - begin),
                z_send_sem.at[n, o],
                (right_sem if to_right else left_sem).at[n, o],
                along((z + 1) % depth) if to_right else along((z + last) % depth),
            )

        def inbox_rows(n, begin, size):
            slot = begin // flat
            return inbox.at[n, slot, pl.ds(begin - slot * flat, size), :]

        def packed_left(n):
            for o in range(len(pieces)):
                packed_copy(n, o, True).wait_send()

    for at in range(0, turned.shape[1], 512):
        turned[:, at : at + 512] = jnp.zeros((half, 512), BF16)
    int_copy(1 - core).wait_recv()

    farther = jnp.maximum(z, last - z)
    dense_right = (z > 0) if not pack else (z > 1)
    dense_left = (z < last) if not pack else (z < last - 1)

    def add_into(n, d, slot):
        part[n, d] = (part[n, d].astype(F32) + inbox[n, slot].astype(F32)).astype(BF16)

    def ladder_step(t):
        a_arrived(t).wait()
        pl.when(t + AHEAD < chunks)(lambda: send_amplitudes(t + AHEAD))
        dress(t)

        def ladder(k, carry):
            d = jnp.where(z * 2 < depth, last - k, k)
            y = dot(tau[...], ints[d]).astype(BF16)
            for k in range(s.tiles):
                part[t, d, k * s.rows : (k + 1) * s.rows, :] = y[:, k * TILE : (k + 1) * TILE]
            if not pack:
                pl.when((z == 0) & (d > 0))(lambda: right_copy(t, d).start())
                pl.when((z == last) & (d < last))(lambda: left_copy(t, d).start())
            return carry

        lax.fori_loop(0, depth, ladder, 0)
        if pack:

            @pl.when((z == 0) | (z == last))
            def _():
                pl.when(t >= 2)(lambda: packed_left(t - 2))
                first = jnp.where(z == 0, 1, 0)
                x = part[t, pl.ds(first, depth - 1)].reshape(s.sent, TILE)
                for o, (begin, end) in enumerate(pieces):
                    packed[t % 2, begin:end, :] = dot(choose[begin:end, :], x).astype(BF16)
                    pl.when(z == 0)(lambda: packed_copy(t, o, True).start())
                    pl.when(z == last)(lambda: packed_copy(t, o, False).start())

        a_left(t).wait()
        ready = t + AHEAD + 1
        pl.when((ready < chunks) & (ready % s.per_load == 0))(
            lambda: prepare(ready // s.per_load)
        )

    def unpack_step(m, to_right):
        base = 2 if to_right else 0
        for o in range(depth - 1):
            if o < len(pieces):
                packed_copy(m, o, to_right).wait_recv()
            end = pieces[min(o, len(pieces) - 1)][1]
            x = [
                inbox[m, base + p, : b_end - b_begin, :]
                for p, (b_begin, b_end) in enumerate(pieces[: o + 1])
            ]
            x = jnp.concatenate(x, axis=0) if len(x) > 1 else x[0]
            k = depth - 2 - o if to_right else o
            d = k + 1 if to_right else k
            y = dot(choose[k * flat : (k + 1) * flat, :end], x)
            part[m, d] = (part[m, d].astype(F32) + y).astype(BF16)
            if to_right and d > 1:
                right_copy(m, d).start()
            if not to_right and d < depth - 2:
                left_copy(m, d).start()

    def right_step(m):
        def pass_on(k, carry):
            d = last - k
            right_copy(m, d).wait_recv()
            add_into(m, d, d + 1)
            right_copy(m, d).start()
            return carry

        lax.fori_loop(0, last - z, pass_on, 0)

    def left_step(m):
        def pass_on(d, carry):
            left_copy(m, d).wait_recv()
            add_into(m, d, d)
            left_copy(m, d).start()
            return carry

        lax.fori_loop(0, z, pass_on, 0)

    def last_step(m):
        acc[...] = part[m, z].astype(F32)

        @pl.when(dense_right)
        def _():
            right_copy(m, z).wait_recv()
            acc[...] += inbox[m, z + 1].astype(F32)

        @pl.when(dense_left)
        def _():
            left_copy(m, z).wait_recv()
            acc[...] += inbox[m, z].astype(F32)

        for k in range(s.tiles):
            c_send[m, :, k * TILE : (k + 1) * TILE] = acc[k * s.rows : (k + 1) * s.rows, :].astype(
                BF16
            )
        each_peer(lambda to: c_copy(m, to).start())
        c_own(m).start()

    def turn_step(u):
        for k in range(s.per_load):
            c_arrived(u * s.per_load + k).wait()
        span = s.sub_i * s.occ
        r = iota((s.count, 1), 0)
        spot = ((r // pair) % s.sub_i) * s.occ + (r // (pair * s.sub_i)) * pair + r % pair
        per = s.sub_j // pair
        for gj in range(s.load // s.sub_j):
            place_j = one_hot(iota((s.count, span), 1) - (u * s.load + gj * s.sub_j) == spot)
            for gi in range(s.firsts // s.sub_i):
                pieces = []
                begin = gj * per
                while begin < (gj + 1) * per:
                    end = min((gj + 1) * per, (begin // group + 1) * group)
                    k = begin // group
                    pieces.append(
                        c_recv[
                            u * s.per_load + k,
                            begin - k * group : end - k * group,
                            gi * s.sub_i * pair : (gi + 1) * s.sub_i * pair,
                            :,
                        ]
                    )
                    begin = end
                x = jnp.concatenate(pieces, axis=0) if len(pieces) > 1 else pieces[0]
                x = x.reshape(s.count, half).T
                step = min(512, span)
                for at in range(0, span, step):
                    y = dot(x, place_j[:, at : at + step]).astype(BF16)
                    cols_at = gi * span + at
                    turned[:, cols_at : cols_at + step] = turned[:, cols_at : cols_at + step] + y

    def step(t, carry):
        pl.when(t < chunks)(lambda: ladder_step(t))

        m = t - z
        live = (m >= 0) & (m < chunks)
        if pack:
            pl.when((z == 1) & live)(lambda: unpack_step(m, True))
        pl.when(dense_right & live)(lambda: right_step(m))

        m_left = t - (last - z)
        live_left = (m_left >= 0) & (m_left < chunks)
        if pack:
            pl.when((z == last - 1) & live_left)(lambda: unpack_step(m_left, False))
        pl.when(dense_left & live_left)(lambda: left_step(m_left))

        m_last = t - farther
        pl.when((m_last >= 0) & (m_last < chunks))(lambda: last_step(m_last))

        m_out = t - farther - 1
        whole = m_out % s.per_load == s.per_load - 1
        pl.when((m_out >= 0) & (m_out < chunks) & whole)(lambda: turn_step(m_out // s.per_load))

        return carry

    lax.fori_loop(0, chunks + depth, step, 0)

    out_copy = pltpu.make_async_copy(turned, out_hbm, out_sem)
    out_copy.start()
    if pack:

        @pl.when(z > 1)
        def _():
            right_spot(spots).wait_recv()
            pl.when(z < last)(lambda: right_spot(right_spots).start())

        @pl.when(z < last - 1)
        def _():
            left_spot(spots).wait_recv()
            pl.when(z > 0)(lambda: left_spot(left_spots).start())

        pl.when(z < last)(lambda: right_spot(spots).wait_send())
        pl.when(z > 0)(lambda: left_spot(spots).wait_send())
        rows = slice(LEAST, LEAST + 8)
        from_left = jnp.where(z == 0, spots[rows, :], right_spots[rows, :])
        from_right = jnp.where(z == last, spots[rows, :], left_spots[rows, :])
        flag_ref[...] = jnp.maximum(from_left, from_right)
        int_map_copy(core).wait_send()

        @pl.when((z == 0) | (z == last))
        def _():
            for n in range(max(0, chunks - 2), chunks):
                packed_left(n)

    else:
        flag_ref[...] = jnp.zeros(flag_ref.shape, F32)

    each_peer(lambda to: map_copy(to, me).wait_send())
    int_copy(core).wait_send()
    dense_sender = jnp.where((z > 0) & (z < last), True, not pack)

    def finish(n, carry):
        def sent(d, carry):
            pl.when((d != z) & dense_sender)(lambda: right_copy(n, d).wait_send())
            return carry

        lax.fori_loop(0, depth, sent, 0)
        c_left(n).wait()
        return carry

    lax.fori_loop(0, chunks, finish, 0)
    out_copy.wait()


def residual(s, pack, amplitudes, amp_tiles, occ_coupling, integrals, int_tiles):
    vmem, dma = pltpu.VMEM, pltpu.SemaphoreType.DMA
    any_space = pl.BlockSpec(memory_space=pl.ANY)
    in_vmem = pl.BlockSpec(memory_space=pltpu.VMEM)
    chunks, depth, group = s.chunks, s.depth, s.group
    both = CORES * s.cols
    scratch = [
        vmem((2, s.firsts, s.load, s.cols), BF16),
        vmem((s.slots, s.per_load * group, s.block, s.cols), BF16),
        vmem((chunks, s.rows, both), BF16),
        vmem((s.rows, both), BF16),
        vmem((s.rows, both), BF16),
        vmem(amp_tiles.shape, jnp.int32),
        vmem(int_tiles.shape, jnp.int32),
        vmem((s.firsts, TILE), F32),
        vmem((s.occ, CORES * TILE), F32),
        vmem((depth, both, s.width), BF16),
        vmem((chunks, depth, s.flat, TILE), BF16),
        vmem((chunks, depth + 1, s.flat, TILE), BF16),
        vmem((s.flat, TILE), F32),
        vmem((chunks, s.rows, s.width), BF16),
        vmem((chunks, group, s.block, s.half), BF16),
        vmem((s.half, s.firsts * s.occ), BF16),
        vmem((s.count, s.count), BF16),
        vmem((s.rows, s.rows), BF16),
        dma((2,)),
        dma((2,)),
        dma((chunks,)),
        dma((chunks,)),
        dma((group,)),
        dma((group,)),
        dma((depth,)),
        dma(()),
        dma(()),
        dma((chunks, depth)),
        dma((chunks, depth)),
        dma((chunks, depth)),
        dma((chunks,)),
        dma((chunks,)),
        dma(()),
    ]
    if pack:
        scratch += [
            vmem((s.sent, s.sent), BF16),
            vmem((2, s.room, TILE), BF16),
            vmem((LEAST + 8, TILE), F32),
            vmem((LEAST + 8, TILE), F32),
            vmem((LEAST + 8, TILE), F32),
            vmem((CORES * (s.cols // TILE), TILE), F32),
            dma((2,)),
            dma(()),
            dma(()),
            dma(()),
            dma(()),
        ]
    return pl.pallas_call(
        functools.partial(residual_kernel, s, pack),
        out_shape=(
            jax.ShapeDtypeStruct((s.half, s.firsts * s.occ), BF16),
            jax.ShapeDtypeStruct((8, TILE), F32),
        ),
        in_specs=[any_space, any_space, in_vmem, any_space, any_space],
        out_specs=(any_space, in_vmem),
        scratch_shapes=scratch,
        compiler_params=pltpu.CompilerParams(
            collective_id=1 if pack else 0,
            has_side_effects=True,
            vmem_limit_bytes=58 * 1024 * 1024,
        ),
        name="packed" if pack else "dense",
    )(
        amplitudes.reshape(s.firsts, s.occ, s.cols),
        amp_tiles,
        occ_coupling,
        integrals,
        int_tiles,
    )


def shards(mesh_shape, *arrays):
    s = Sizes(mesh_shape, arrays[0], arrays[2], arrays[3])
    if PACK and s.can_pack:
        out, used = residual(s, True, *arrays)
        return lax.cond(
            used[0, 0] > s.room, lambda: residual(s, False, *arrays)[0], lambda: out
        )
    return residual(s, False, *arrays)[0]


PACK = True


def solution(mesh):
    shape = mesh.devices.shape
    in_specs = (P("bulk", "cuts"), P("bulk", "cuts"), P(), P("cuts", None), P("cuts", None))
    return jax.shard_map(
        functools.partial(shards, shape),
        mesh=mesh,
        in_specs=in_specs,
        out_specs=P("cuts", "bulk"),
        check_vma=False,
    )
```

```python
import functools

import jax
import jax.numpy as jnp
from jax import lax
from jax.experimental import pallas as pl
from jax.experimental.pallas import tpu as pltpu
from jax.sharding import PartitionSpec as P

TILE = 128
CORES = 2
LEAST = 16
BLOCK = 256
AHEAD = 2
PARTS = 1
MESH = pl.DeviceIdType.MESH
F32 = jnp.float32
BF16 = jnp.bfloat16


def dot(a, b):
    return jnp.dot(a, b, preferred_element_type=F32)


def iota(shape, axis):
    return lax.broadcasted_iota(jnp.int32, shape, axis)


def one_hot(condition):
    return jnp.where(condition, 1.0, 0.0).astype(BF16)


class Sizes:
    def __init__(self, mesh_shape, amplitudes, occ_coupling, integrals):
        self.bulk, cuts = mesh_shape
        self.depth = cuts // CORES
        self.group = self.bulk * CORES
        local_rows, self.cols = amplitudes.shape
        self.occ = occ_coupling.shape[0]
        self.firsts = local_rows // self.occ
        self.pair = max(1, LEAST // self.firsts)
        self.seconds = self.pair * self.group
        self.chunks = self.occ // self.seconds
        self.load = max(LEAST, self.seconds)
        self.per_load = self.load // self.seconds
        self.loads = self.occ // self.load
        self.slots = 3 if self.per_load > 1 else AHEAD + 2
        self.width = integrals.shape[1] // self.depth
        self.half = self.width // CORES
        self.rows = self.pair * self.occ
        self.block = self.firsts * self.pair
        self.sub_j = min(self.load, max(LEAST, BLOCK // self.firsts))
        self.sub_i = min(self.firsts, BLOCK // self.sub_j)
        self.count = self.sub_i * self.sub_j
        self.tiles = self.width // TILE
        self.flat = self.tiles * self.rows
        self.piece = self.flat // PARTS
        self.sent = (self.depth - 1) * self.flat
        self.can_pack = self.pair == 1 and self.depth == 4 and self.occ == TILE
        self.room = self.sent * 26 // 32 // LEAST * LEAST


def residual_kernel(s, pack, *refs):
    (
        amp_hbm,
        tiles_hbm,
        occ_ref,
        int_hbm,
        int_tiles_hbm,
        turned,
        flag_ref,
        x_buf,
        send_buf,
        slab,
        tau,
        mask,
        tiles_ref,
        int_tiles_ref,
        map_send,
        map_recv,
        ints,
        part,
        inbox,
        acc,
        c_send,
        c_recv,
        split_rows,
        chosen,
        mix,
        x_sem,
        tiles_sem,
        a_send_sem,
        a_recv_sem,
        map_send_sem,
        map_recv_sem,
        int_local_sem,
        int_send_sem,
        int_recv_sem,
        z_send_sem,
        right_sem,
        left_sem,
        c_send_sem,
        c_recv_sem,
    ) = refs[:39]
    if pack:
        (
            choose,
            packed,
            spots,
            right_spots,
            left_spots,
            int_map,
            spot_send_sem,
            right_spot_sem,
            left_spot_sem,
            int_map_send_sem,
            int_map_recv_sem,
        ) = refs[39:]
    depth, group, chunks, cols, pair = s.depth, s.group, s.chunks, s.cols, s.pair
    block, half, flat, piece = s.block, s.half, s.flat, s.piece
    b = lax.axis_index("bulk")
    cut = lax.axis_index("cuts")
    z = cut // CORES
    core = cut % CORES
    me = b * CORES + core
    last = depth - 1

    def aligned(start, size):
        return pl.ds(pl.multiple_of(start, size), size)

    def at_rank(rank):
        return (rank // CORES, z * CORES + rank % CORES)

    def along(zz):
        return (b, zz * CORES + core)

    def remote(src, dst, send_sem, recv_sem, device):
        return pltpu.make_async_remote_copy(
            src_ref=src,
            dst_ref=dst,
            send_sem=send_sem,
            recv_sem=recv_sem,
            device_id=device,
            device_id_type=MESH,
        )

    def each_peer(body):
        def step(k, carry):
            body((me + k) % group)
            return carry

        lax.fori_loop(1, group, step, 0)

    def x_copy(u):
        return pltpu.make_async_copy(
            amp_hbm.at[:, aligned(u * s.load, s.load), :], x_buf.at[u % 2], x_sem.at[u % 2]
        )

    def place(n, rank):
        return slab.at[n, aligned((rank // CORES) * block, block), aligned((rank % CORES) * cols, cols)]

    def outgoing(n, to):
        return send_buf.at[(n // s.per_load) % s.slots, (n % s.per_load) * group + to]

    def a_copy(n, to):
        return remote(
            outgoing(n, to), place(n, me), a_send_sem.at[n], a_recv_sem.at[n], at_rank(to)
        )

    def a_arrived(n):
        return pltpu.make_async_copy(slab.at[n], slab.at[n], a_recv_sem.at[n])

    def a_left(n):
        ref = send_buf.at[(n // s.per_load) % s.slots, pl.ds((n % s.per_load) * group, group - 1)]
        return pltpu.make_async_copy(ref, ref, a_send_sem.at[n])

    def map_place(source):
        return map_recv.at[
            aligned((source // CORES) * s.firsts, s.firsts), aligned((source % CORES) * TILE, TILE)
        ]

    def map_copy(to, source):
        return remote(
            map_send, map_place(source), map_send_sem.at[to], map_recv_sem.at[source], at_rank(to)
        )

    def int_local(d):
        return pltpu.make_async_copy(
            int_hbm.at[:, aligned(d * s.width, s.width)],
            ints.at[d, aligned(core * cols, cols), :],
            int_local_sem.at[d],
        )

    def int_copy(d, source):
        return remote(
            ints.at[d, aligned(core * cols, cols), :],
            ints.at[d, aligned(source * cols, cols), :],
            int_send_sem.at[d],
            int_recv_sem.at[d],
            at_rank(b * CORES + 1 - core),
        )

    def right_copy(n, d, h):
        span = pl.ds(h * piece, piece)
        return remote(
            part.at[n, d, span],
            inbox.at[n, d + 1, span],
            z_send_sem.at[n, d * PARTS + h],
            right_sem.at[n, d * PARTS + h],
            along((z + 1) % depth),
        )

    def left_copy(n, d, h):
        span = pl.ds(h * piece, piece)
        return remote(
            part.at[n, d, span],
            inbox.at[n, d, span],
            z_send_sem.at[n, d * PARTS + h],
            left_sem.at[n, d * PARTS + h],
            along((z + last) % depth),
        )

    def c_copy(n, to):
        return remote(
            c_send.at[n, aligned((to // CORES) * block, block), aligned((to % CORES) * half, half)],
            c_recv.at[n, me],
            c_send_sem.at[n],
            c_recv_sem.at[n],
            at_rank(to),
        )

    def c_own(n):
        return pltpu.make_async_copy(
            c_send.at[n, aligned(b * block, block), aligned(core * half, half)],
            c_recv.at[n, me],
            c_recv_sem.at[n],
        )

    def c_arrived(n):
        return pltpu.make_async_copy(c_recv.at[n], c_recv.at[n], c_recv_sem.at[n])

    def c_left(n):
        ref = c_recv.at[n, pl.ds(0, group - 1)]
        return pltpu.make_async_copy(ref, ref, c_send_sem.at[n])

    def prepare(u):
        x_copy(u).wait()
        for gi in range(s.firsts // s.sub_i):
            for gj in range(s.load // s.sub_j):
                x = x_buf[
                    u % 2,
                    gi * s.sub_i : (gi + 1) * s.sub_i,
                    gj * s.sub_j : (gj + 1) * s.sub_j,
                    :,
                ]
                y = dot(split_rows[...], x.reshape(s.count, cols)).astype(BF16)
                send_buf[
                    u % s.slots,
                    gj * s.sub_j // pair : (gj + 1) * s.sub_j // pair,
                    gi * s.sub_i * pair : (gi + 1) * s.sub_i * pair,
                    :,
                ] = y.reshape(s.sub_j // pair, s.sub_i * pair, cols)
        pl.when(u + 2 < s.loads)(lambda: x_copy(u + 2).start())

    def send_amplitudes(n):
        each_peer(lambda to: a_copy(n, to).start())
        pltpu.make_async_copy(outgoing(n, me), place(n, me), a_recv_sem.at[n]).start()

    def dress(n):
        span = min(512, CORES * cols)
        for at in range(0, CORES * cols, span):
            kept = mask[:, at : at + span]
            masked = slab[n, :, at : at + span] * kept
            mixed = dot(mix[...], masked)
            dressed = (masked.astype(F32) + mixed).astype(BF16)
            tau[:, at : at + span] = dressed * kept

    def in_turn(k):
        return jnp.where(z * 2 < depth, last - k, k)

    tiles_copy = pltpu.make_async_copy(tiles_hbm, tiles_ref, tiles_sem.at[0])
    int_tiles_copy = pltpu.make_async_copy(int_tiles_hbm, int_tiles_ref, tiles_sem.at[1])
    x_copy(0).start()
    tiles_copy.start()
    int_tiles_copy.start()
    barrier = pltpu.get_barrier_semaphore()

    def greet(device):
        pl.semaphore_signal(barrier, inc=1, device_id=device, device_id_type=MESH)

    each_peer(lambda to: greet(at_rank(to)))
    pl.when(z > 0)(lambda: greet(along(z - 1)))
    pl.when(z < last)(lambda: greet(along(z + 1)))
    for k in range(depth):
        int_local(in_turn(k)).start()
    if s.loads > 1:
        x_copy(1).start()

    r, c = iota((s.count, 1), 0), iota((1, s.count), 1)
    natural = ((r // pair) % s.sub_i) * s.sub_j + (r // (pair * s.sub_i)) * pair + r % pair
    split_rows[...] = one_hot(c == natural)
    prepare(0)
    tiles_copy.wait()
    int_tiles_copy.wait()
    kept_tiles = tiles_ref[...].astype(F32)
    kept_tiles = jnp.concatenate(
        [kept_tiles, jnp.zeros((kept_tiles.shape[0], TILE - s.firsts), F32)], axis=1
    )
    kept_tiles = jnp.concatenate(
        [kept_tiles, jnp.zeros((TILE - kept_tiles.shape[0], TILE), F32)], axis=0
    )
    map_send[...] = kept_tiles.T[: s.firsts]
    own_tiles = cols // TILE
    if pack:
        int_tiles = int_tiles_ref[...].astype(F32)
        int_map[aligned(core * own_tiles, own_tiles), :] = jnp.concatenate(
            [int_tiles, jnp.zeros((own_tiles, TILE - int_tiles.shape[1]), F32)], axis=1
        )

    def mask_ints(k):
        d = in_turn(k)
        int_local(d).wait()
        tiles = int_tiles_ref.shape[1]
        spread = one_hot(
            iota((1, s.width), 1) // TILE == iota((tiles, 1), 0) - d * s.tiles
        )
        kept = dot(int_tiles_ref[...].astype(F32).astype(BF16), spread).astype(BF16)
        for j in range(own_tiles):
            span = aligned(core * cols + j * TILE, TILE)
            ints[d, span, :] = ints[d, span, :] * kept[j : j + 1, :]

    mask_ints(0)

    ends = jnp.where(z > 0, 1, 0) + jnp.where(z < last, 1, 0)
    pl.semaphore_wait(barrier, group - 1 + ends)

    each_peer(lambda to: map_copy(to, me).start())
    own_map = pltpu.make_async_copy(map_send, map_place(me), map_recv_sem.at[me])
    own_map.start()
    if pack:

        def int_map_copy(source):
            span = aligned(source * own_tiles, own_tiles)
            mine = aligned(core * own_tiles, own_tiles)
            return remote(
                int_map.at[mine],
                int_map.at[span],
                int_map_send_sem,
                int_map_recv_sem,
                at_rank(b * CORES + 1 - core),
            )

        int_map_copy(core).start()
    send_amplitudes(0)

    int_copy(in_turn(0), core).start()

    def mask_more(k, carry):
        mask_ints(k)
        int_copy(in_turn(k), core).start()
        return carry

    lax.fori_loop(1, depth, mask_more, 0)
    for n in range(1, min(AHEAD + 1, chunks)):
        if n % s.per_load == 0:
            prepare(n // s.per_load)
        if n < AHEAD:
            send_amplitudes(n)
    tall = one_hot(iota((s.rows, s.occ), 0) // pair == iota((s.rows, s.occ), 1))
    if pair == 1:
        mix[...] = occ_ref[...]
    else:
        wide = one_hot(iota((s.occ, s.rows), 1) // pair == iota((s.occ, s.rows), 0))
        stretched = dot(dot(tall, occ_ref[...]).astype(BF16), wide)
        same = iota((s.rows, s.rows), 0) % pair == iota((s.rows, s.rows), 1) % pair
        mix[...] = jnp.where(same, stretched, 0.0).astype(BF16)

    own_map.wait()
    each_peer(lambda source: map_copy(source, source).wait_recv())
    tiles_all = dot(tall, map_recv[...].astype(BF16)).astype(BF16)
    lane = iota((CORES * TILE, 1), 0)
    col = iota((1, CORES * cols), 1)
    mask[...] = dot(
        tiles_all, one_hot(lane == (col // cols) * TILE + (col % cols) // TILE)
    ).astype(BF16)

    if pack:
        others = (depth - 1) * s.tiles
        room = s.room

        def spot_copy(src, sem, dst, recv, device):
            return remote(src, dst, sem, recv, device)

        def right_spot(src):
            return remote(
                src, right_spots, spot_send_sem.at[0], right_spot_sem, along((z + 1) % depth)
            )

        def left_spot(src):
            return remote(
                src, left_spots, spot_send_sem.at[1], left_spot_sem, along((z + last) % depth)
            )

        int_map_copy(1 - core).wait_recv()

        @pl.when((z == 0) | (z == last))
        def _():
            hits = jnp.zeros((s.occ, TILE), F32)
            for k in range(CORES):
                rows = int_map[k * own_tiles : (k + 1) * own_tiles, :]
                rows = jnp.concatenate([rows, jnp.zeros((TILE - own_tiles, TILE), F32)], axis=0)
                hits += dot(
                    map_recv[:, k * TILE : (k + 1) * TILE].astype(BF16), rows.astype(BF16)
                )
            hits = jnp.where(hits > 0.5, 1.0, 0.0).T
            hits = jnp.where(z == 0, hits[s.tiles : s.tiles + others], hits[:others])
            hits = jnp.concatenate([hits, jnp.zeros((LEAST - others, TILE), F32)], axis=0)
            marks = hits.astype(BF16)
            i, k = iota((TILE, TILE), 0), iota((TILE, TILE), 1)
            ahead = dot(marks, one_hot(i < k))
            totals = dot(marks, jnp.ones((TILE, TILE), BF16))
            r, c = iota((LEAST, LEAST), 0), iota((LEAST, LEAST), 1)
            before = jnp.where(z == 0, one_hot(c > r), one_hot(c < r))
            ahead += dot(before, totals.astype(BF16))
            spots[0:LEAST, :] = jnp.where(hits > 0.5, ahead, -1.0)
            total = jnp.sum(hits, axis=0, keepdims=True)
            total = jnp.sum(total, axis=1, keepdims=True)
            spots[LEAST:, :] = jnp.broadcast_to(total, (spots.shape[0] - LEAST, TILE))
            pl.when(z == 0)(lambda: right_spot(spots).start())
            pl.when(z == last)(lambda: left_spot(spots).start())
            at = iota((room, TILE), 0).astype(F32)
            for k in range(others):
                choose[0:room, k * TILE : (k + 1) * TILE] = one_hot(at == spots[k : k + 1, :])

        def restore(ref):
            where = jnp.concatenate(
                [ref[0:LEAST, :], jnp.full((TILE - LEAST, TILE), -1.0, F32)], axis=0
            ).T
            at = iota((TILE, room), 1).astype(F32)
            for k in range(others):
                choose[k * TILE : (k + 1) * TILE, 0:room] = one_hot(at == where[:, k : k + 1])

        @pl.when(z == 1)
        def _():
            right_spot(spots).wait_recv()
            right_spot(right_spots).start()

        @pl.when(z == last - 1)
        def _():
            left_spot(spots).wait_recv()
            left_spot(left_spots).start()

        pieces = []
        for begin in range(0, room, piece):
            pieces.append((begin, min(room, begin + piece)))

        def packed_copy(n, o, to_right):
            begin, end = pieces[o]
            base = 2 * flat if to_right else 0
            return remote(
                packed.at[n % 2, pl.ds(begin, end - begin), :],
                inbox_rows(n, base + begin, end - begin),
                z_send_sem.at[n, o],
                (right_sem if to_right else left_sem).at[n, o],
                along((z + 1) % depth) if to_right else along((z + last) % depth),
            )

        def inbox_rows(n, begin, size):
            slot = begin // flat
            return inbox.at[n, slot, pl.ds(begin - slot * flat, size), :]

        def packed_left(n):
            for o in range(len(pieces)):
                packed_copy(n, o, True).wait_send()


    farther = jnp.maximum(z, last - z)
    dense_right = (z > 0) if not pack else (z > 1)
    dense_left = (z < last) if not pack else (z < last - 1)

    def add_into(n, d, slot, h):
        rows = slice(h * piece, (h + 1) * piece)
        total = part[n, d, rows, :].astype(F32) + inbox[n, slot, rows, :].astype(F32)
        part[n, d, rows, :] = total.astype(BF16)

    def ladder_step(t):
        a_arrived(t).wait()
        pl.when(t + AHEAD < chunks)(lambda: send_amplitudes(t + AHEAD))
        dress(t)

        def ladder(k, carry):
            d = in_turn(k)
            pl.when(t == 0)(lambda: int_copy(d, 1 - core).wait_recv())
            y = dot(tau[...], ints[d]).astype(BF16)
            for k in range(s.tiles):
                part[t, d, k * s.rows : (k + 1) * s.rows, :] = y[:, k * TILE : (k + 1) * TILE]
            if not pack:
                for h in range(PARTS):
                    pl.when((z == 0) & (d > 0))(lambda: right_copy(t, d, PARTS - 1 - h).start())
                    pl.when((z == last) & (d < last))(lambda: left_copy(t, d, h).start())
            return carry

        lax.fori_loop(0, depth, ladder, 0)
        if pack:

            @pl.when((z == 0) | (z == last))
            def _():
                pl.when(t >= 2)(lambda: packed_left(t - 2))
                first = jnp.where(z == 0, 1, 0)
                x = part[t, pl.ds(first, depth - 1)].reshape(s.sent, TILE)
                for o, (begin, end) in enumerate(pieces):
                    if begin % flat == 0:
                        until = min(room, begin + flat)
                        packed[t % 2, begin:until, :] = dot(choose[begin:until, :], x).astype(BF16)
                    pl.when(z == 0)(lambda: packed_copy(t, o, True).start())
                    pl.when(z == last)(lambda: packed_copy(t, o, False).start())

        a_left(t).wait()

        @pl.when(t == 0)
        def _():
            for at in range(0, turned.shape[1], 512):
                turned[:, at : at + 512] = jnp.zeros((half, 512), BF16)
            if pack:
                pl.when(z == 1)(lambda: restore(right_spots))
                pl.when(z == last - 1)(lambda: restore(left_spots))

        ready = t + AHEAD + 1
        pl.when((ready < chunks) & (ready % s.per_load == 0))(
            lambda: prepare(ready // s.per_load)
        )

    def unpack_step(m, to_right):
        base = 2 if to_right else 0
        count = (depth - 1) * PARTS
        x = []
        for o in range(count):
            if o < len(pieces):
                packed_copy(m, o, to_right).wait_recv()
                begin, end = pieces[o]
                rows = slice(begin % flat, begin % flat + end - begin)
                x.append(inbox[m, base + begin // flat, rows, :])
            g = count - 1 - o if to_right else o
            d, h = g // PARTS + (1 if to_right else 0), g % PARTS
            y = dot(choose[g * piece : (g + 1) * piece, :end], jnp.concatenate(x, axis=0))
            rows = slice(h * piece, (h + 1) * piece)
            part[m, d, rows, :] = (part[m, d, rows, :].astype(F32) + y).astype(BF16)
            if to_right and d > 1:
                right_copy(m, d, h).start()
            if not to_right and d < depth - 2:
                left_copy(m, d, h).start()

    def right_step(m):
        def pass_on(k, carry):
            d = last - k
            for h in reversed(range(PARTS)):
                right_copy(m, d, h).wait_recv()
                add_into(m, d, d + 1, h)
                right_copy(m, d, h).start()
            return carry

        lax.fori_loop(0, last - z, pass_on, 0)

    def left_step(m):
        def pass_on(d, carry):
            for h in range(PARTS):
                left_copy(m, d, h).wait_recv()
                add_into(m, d, d, h)
                left_copy(m, d, h).start()
            return carry

        lax.fori_loop(0, z, pass_on, 0)

    def last_step(m):
        acc[...] = part[m, z].astype(F32)

        @pl.when(dense_right)
        def _():
            for h in range(PARTS):
                right_copy(m, z, h).wait_recv()
            acc[...] += inbox[m, z + 1].astype(F32)

        @pl.when(dense_left)
        def _():
            for h in range(PARTS):
                left_copy(m, z, h).wait_recv()
            acc[...] += inbox[m, z].astype(F32)

        for k in range(s.tiles):
            c_send[m, :, k * TILE : (k + 1) * TILE] = acc[k * s.rows : (k + 1) * s.rows, :].astype(
                BF16
            )
        each_peer(lambda to: c_copy(m, to).start())
        c_own(m).start()

    def turn_step(u):
        span = s.sub_i * s.occ
        r = iota((s.count, 1), 0)
        spot = ((r // pair) % s.sub_i) * s.occ + (r // (pair * s.sub_i)) * pair + r % pair
        per = s.sub_j // pair
        for gj in range(s.load // s.sub_j):
            shift = u * s.load + gj * s.sub_j
            chosen[...] = one_hot(iota((1, span), 1) - shift == spot)
            if gj == 0:
                for k in range(s.per_load):
                    c_arrived(u * s.per_load + k).wait()
            for gi in range(s.firsts // s.sub_i):
                pieces = []
                begin = gj * per
                while begin < (gj + 1) * per:
                    end = min((gj + 1) * per, (begin // group + 1) * group)
                    k = begin // group
                    pieces.append(
                        c_recv[
                            u * s.per_load + k,
                            begin - k * group : end - k * group,
                            gi * s.sub_i * pair : (gi + 1) * s.sub_i * pair,
                            :,
                        ]
                    )
                    begin = end
                x = jnp.concatenate(pieces, axis=0) if len(pieces) > 1 else pieces[0]
                x = x.reshape(s.count, half).T
                step = min(512, span)
                for at in range(0, span, step):
                    y = dot(x, chosen[:, at : at + step]).astype(BF16)
                    cols_at = gi * span + at
                    turned[:, cols_at : cols_at + step] = turned[:, cols_at : cols_at + step] + y

    def step(t, carry):
        pl.when(t < chunks)(lambda: ladder_step(t))

        m = t - z
        live = (m >= 0) & (m < chunks)
        m_left = t - (last - z)
        live_left = (m_left >= 0) & (m_left < chunks)
        m_last = t - farther
        m_out = m_last - 1
        whole = (m_out >= 0) & (m_out < chunks) & (m_out % s.per_load == s.per_load - 1)

        def unpack(when):
            pl.when((z == 1) & live & when)(lambda: unpack_step(m, True))
            pl.when((z == last - 1) & live_left & when)(lambda: unpack_step(m_left, False))

        if pack:
            unpack(t < chunks)
        pl.when(dense_right & live)(lambda: right_step(m))
        pl.when(dense_left & live_left)(lambda: left_step(m_left))
        pl.when((m_last >= 0) & (m_last < chunks))(lambda: last_step(m_last))
        if pack:
            unpack(t >= chunks)
        pl.when(whole)(lambda: turn_step(m_out // s.per_load))

        return carry

    lax.fori_loop(0, chunks + depth, step, 0)

    if pack:

        @pl.when(z > 1)
        def _():
            right_spot(spots).wait_recv()
            pl.when(z < last)(lambda: right_spot(right_spots).start())

        @pl.when(z < last - 1)
        def _():
            left_spot(spots).wait_recv()
            pl.when(z > 0)(lambda: left_spot(left_spots).start())

        pl.when(z < last)(lambda: right_spot(spots).wait_send())
        pl.when(z > 0)(lambda: left_spot(spots).wait_send())
        rows = slice(LEAST, LEAST + 8)
        from_left = jnp.where(z == 0, spots[rows, :], right_spots[rows, :])
        from_right = jnp.where(z == last, spots[rows, :], left_spots[rows, :])
        flag_ref[0, 0] = jnp.max(jnp.maximum(from_left, from_right))
        int_map_copy(core).wait_send()

        @pl.when((z == 0) | (z == last))
        def _():
            for n in range(max(0, chunks - 2), chunks):
                packed_left(n)

    else:
        flag_ref[0, 0] = jnp.float32(0)

    each_peer(lambda to: map_copy(to, me).wait_send())
    for d in range(depth):
        int_copy(d, core).wait_send()
    dense_sender = jnp.where((z > 0) & (z < last), True, not pack)

    def finish(n, carry):
        def sent(d, carry):
            for h in range(PARTS):
                pl.when((d != z) & dense_sender)(lambda: right_copy(n, d, h).wait_send())
            return carry

        lax.fori_loop(0, depth, sent, 0)
        c_left(n).wait()
        return carry

    lax.fori_loop(0, chunks, finish, 0)


def residual(s, pack, amplitudes, amp_tiles, occ_coupling, integrals, int_tiles):
    vmem, dma = pltpu.VMEM, pltpu.SemaphoreType.DMA
    any_space = pl.BlockSpec(memory_space=pl.ANY)
    in_vmem = pl.BlockSpec(memory_space=pltpu.VMEM)
    chunks, depth, group = s.chunks, s.depth, s.group
    both = CORES * s.cols
    scratch = [
        vmem((2, s.firsts, s.load, s.cols), BF16),
        vmem((s.slots, s.per_load * group, s.block, s.cols), BF16),
        vmem((chunks, s.rows, both), BF16),
        vmem((s.rows, both), BF16),
        vmem((s.rows, both), BF16),
        vmem(amp_tiles.shape[::-1], jnp.int32),
        vmem(int_tiles.shape, jnp.int32),
        vmem((s.firsts, TILE), F32),
        vmem((s.occ, CORES * TILE), F32),
        vmem((depth, both, s.width), BF16),
        vmem((chunks, depth, s.flat, TILE), BF16),
        vmem((chunks, depth + 1, s.flat, TILE), BF16),
        vmem((s.flat, TILE), F32),
        vmem((chunks, s.rows, s.width), BF16),
        vmem((chunks, group, s.block, s.half), BF16),
        vmem((s.count, s.count), BF16),
        vmem((s.count, s.sub_i * s.occ), BF16),
        vmem((s.rows, s.rows), BF16),
        dma((2,)),
        dma((2,)),
        dma((chunks,)),
        dma((chunks,)),
        dma((group,)),
        dma((group,)),
        dma((depth,)),
        dma((depth,)),
        dma((depth,)),
        dma((chunks, depth * PARTS)),
        dma((chunks, depth * PARTS)),
        dma((chunks, depth * PARTS)),
        dma((chunks,)),
        dma((chunks,)),
    ]
    if pack:
        scratch += [
            vmem((s.sent, s.sent), BF16),
            vmem((2, s.room, TILE), BF16),
            vmem((LEAST + 8, TILE), F32),
            vmem((LEAST + 8, TILE), F32),
            vmem((LEAST + 8, TILE), F32),
            vmem((CORES * (s.cols // TILE), TILE), F32),
            dma((2,)),
            dma(()),
            dma(()),
            dma(()),
            dma(()),
        ]
    return pl.pallas_call(
        functools.partial(residual_kernel, s, pack),
        out_shape=(
            pltpu.VMEM((s.half, s.firsts * s.occ), BF16),
            jax.ShapeDtypeStruct((1, 1), F32),
        ),
        in_specs=[any_space, any_space, in_vmem, any_space, any_space],
        out_specs=(in_vmem, pl.BlockSpec(memory_space=pltpu.SMEM)),
        scratch_shapes=scratch,
        compiler_params=pltpu.CompilerParams(
            collective_id=1 if pack else 0,
            has_side_effects=True,
            vmem_limit_bytes=58 * 1024 * 1024,
        ),
        name="packed" if pack else "dense",
    )(
        amplitudes.reshape(s.firsts, s.occ, s.cols),
        amp_tiles.T,
        occ_coupling,
        integrals,
        int_tiles,
    )


def shards(mesh_shape, *arrays):
    s = Sizes(mesh_shape, arrays[0], arrays[2], arrays[3])
    if PACK and s.can_pack:
        out, used = residual(s, True, *arrays)
        return lax.cond(
            used[0, 0] > s.room, lambda: residual(s, False, *arrays)[0], lambda: out
        )
    return residual(s, False, *arrays)[0]


PACK = True


def solution(mesh):
    shape = mesh.devices.shape
    in_specs = (P("bulk", "cuts"), P("bulk", "cuts"), P(), P("cuts", None), P("cuts", None))
    return jax.shard_map(
        functools.partial(shards, shape),
        mesh=mesh,
        in_specs=in_specs,
        out_specs=P("cuts", "bulk"),
        check_vma=False,
    )
```

```python
import functools

import jax
import jax.numpy as jnp
from jax import lax
from jax.experimental import pallas as pl
from jax.experimental.pallas import tpu as pltpu
from jax.sharding import PartitionSpec as P

TILE = 128
CORES = 2
LEAST = 16
BLOCK = 256
AHEAD = 2
LATE = 5
PARTS = 1
MESH = pl.DeviceIdType.MESH
F32 = jnp.float32
BF16 = jnp.bfloat16


def dot(a, b):
    return jnp.dot(a, b, preferred_element_type=F32)


def iota(shape, axis):
    return lax.broadcasted_iota(jnp.int32, shape, axis)


def one_hot(condition):
    return jnp.where(condition, 1.0, 0.0).astype(BF16)


class Sizes:
    def __init__(self, mesh_shape, amplitudes, occ_coupling, integrals):
        self.bulk, cuts = mesh_shape
        self.depth = cuts // CORES
        self.group = self.bulk * CORES
        local_rows, self.cols = amplitudes.shape
        self.occ = occ_coupling.shape[0]
        self.firsts = local_rows // self.occ
        self.pair = max(1, LEAST // self.firsts)
        self.seconds = self.pair * self.group
        self.chunks = self.occ // self.seconds
        self.load = max(LEAST, self.seconds)
        self.per_load = self.load // self.seconds
        self.loads = self.occ // self.load
        self.slots = 3 if self.per_load > 1 else AHEAD + 2
        self.width = integrals.shape[1] // self.depth
        self.half = self.width // CORES
        self.rows = self.pair * self.occ
        self.block = self.firsts * self.pair
        self.sub_j = min(self.load, max(LEAST, BLOCK // self.firsts))
        self.sub_i = min(self.firsts, BLOCK // self.sub_j)
        self.count = self.sub_i * self.sub_j
        self.tiles = self.width // TILE
        self.flat = self.tiles * self.rows
        self.piece = self.flat // PARTS
        self.sent = (self.depth - 1) * self.flat
        self.can_pack = self.pair == 1 and self.depth == 4 and self.occ == TILE
        self.room = self.sent * 26 // 32 // LEAST * LEAST


def residual_kernel(s, pack, *refs):
    (
        amp_hbm,
        tiles_hbm,
        occ_ref,
        int_hbm,
        int_tiles_hbm,
        turned,
        flag_ref,
        x_buf,
        send_buf,
        slab,
        tau,
        mask,
        tiles_ref,
        int_tiles_ref,
        map_send,
        map_recv,
        ints,
        part,
        inbox,
        acc,
        c_send,
        c_recv,
        split_rows,
        chosen,
        mix,
        x_sem,
        tiles_sem,
        a_send_sem,
        a_recv_sem,
        map_send_sem,
        map_recv_sem,
        int_local_sem,
        int_send_sem,
        int_recv_sem,
        z_send_sem,
        right_sem,
        left_sem,
        c_send_sem,
        c_recv_sem,
    ) = refs[:39]
    if pack:
        (
            choose,
            packed,
            spots,
            right_spots,
            left_spots,
            int_map,
            spot_send_sem,
            right_spot_sem,
            left_spot_sem,
            int_map_send_sem,
            int_map_recv_sem,
        ) = refs[39:]
    depth, group, chunks, cols, pair = s.depth, s.group, s.chunks, s.cols, s.pair
    block, half, flat, piece = s.block, s.half, s.flat, s.piece
    b = lax.axis_index("bulk")
    cut = lax.axis_index("cuts")
    z = cut // CORES
    core = cut % CORES
    me = b * CORES + core
    last = depth - 1

    def aligned(start, size):
        return pl.ds(pl.multiple_of(start, size), size)

    def at_rank(rank):
        return (rank // CORES, z * CORES + rank % CORES)

    def along(zz):
        return (b, zz * CORES + core)

    def remote(src, dst, send_sem, recv_sem, device):
        return pltpu.make_async_remote_copy(
            src_ref=src,
            dst_ref=dst,
            send_sem=send_sem,
            recv_sem=recv_sem,
            device_id=device,
            device_id_type=MESH,
        )

    def each_peer(body):
        def step(k, carry):
            body((me + k) % group)
            return carry

        lax.fori_loop(1, group, step, 0)

    def x_copy(u):
        return pltpu.make_async_copy(
            amp_hbm.at[:, aligned(u * s.load, s.load), :], x_buf.at[u % 2], x_sem.at[u % 2]
        )

    def place(n, rank):
        return slab.at[n, aligned((rank // CORES) * block, block), aligned((rank % CORES) * cols, cols)]

    def outgoing(n, to):
        return send_buf.at[(n // s.per_load) % s.slots, (n % s.per_load) * group + to]

    def a_copy(n, to):
        return remote(
            outgoing(n, to), place(n, me), a_send_sem.at[n], a_recv_sem.at[n], at_rank(to)
        )

    def a_arrived(n):
        return pltpu.make_async_copy(slab.at[n], slab.at[n], a_recv_sem.at[n])

    def a_left(n):
        ref = send_buf.at[(n // s.per_load) % s.slots, pl.ds((n % s.per_load) * group, group - 1)]
        return pltpu.make_async_copy(ref, ref, a_send_sem.at[n])

    def map_place(source):
        return map_recv.at[
            aligned((source // CORES) * s.firsts, s.firsts), aligned((source % CORES) * TILE, TILE)
        ]

    def map_copy(to, source):
        return remote(
            map_send, map_place(source), map_send_sem.at[to], map_recv_sem.at[source], at_rank(to)
        )

    def int_local(d):
        return pltpu.make_async_copy(
            int_hbm.at[:, aligned(d * s.width, s.width)],
            ints.at[d, aligned(core * cols, cols), :],
            int_local_sem.at[d],
        )

    def int_copy(d, source):
        return remote(
            ints.at[d, aligned(core * cols, cols), :],
            ints.at[d, aligned(source * cols, cols), :],
            int_send_sem.at[d],
            int_recv_sem.at[d],
            at_rank(b * CORES + 1 - core),
        )

    def right_copy(n, d, h):
        span = pl.ds(h * piece, piece)
        return remote(
            part.at[n, d, span],
            inbox.at[n, d + 1, span],
            z_send_sem.at[n, d * PARTS + h],
            right_sem.at[n, d * PARTS + h],
            along((z + 1) % depth),
        )

    def left_copy(n, d, h):
        span = pl.ds(h * piece, piece)
        return remote(
            part.at[n, d, span],
            inbox.at[n, d, span],
            z_send_sem.at[n, d * PARTS + h],
            left_sem.at[n, d * PARTS + h],
            along((z + last) % depth),
        )

    def c_copy(n, to):
        return remote(
            c_send.at[n, aligned((to // CORES) * block, block), aligned((to % CORES) * half, half)],
            c_recv.at[n, me],
            c_send_sem.at[n],
            c_recv_sem.at[n],
            at_rank(to),
        )

    def c_own(n):
        return pltpu.make_async_copy(
            c_send.at[n, aligned(b * block, block), aligned(core * half, half)],
            c_recv.at[n, me],
            c_recv_sem.at[n],
        )

    def c_arrived(n):
        return pltpu.make_async_copy(c_recv.at[n], c_recv.at[n], c_recv_sem.at[n])

    def c_left(n):
        ref = c_recv.at[n, pl.ds(0, group - 1)]
        return pltpu.make_async_copy(ref, ref, c_send_sem.at[n])

    def prepare(u):
        x_copy(u).wait()
        for gi in range(s.firsts // s.sub_i):
            for gj in range(s.load // s.sub_j):
                x = x_buf[
                    u % 2,
                    gi * s.sub_i : (gi + 1) * s.sub_i,
                    gj * s.sub_j : (gj + 1) * s.sub_j,
                    :,
                ]
                y = dot(split_rows[...], x.reshape(s.count, cols)).astype(BF16)
                send_buf[
                    u % s.slots,
                    gj * s.sub_j // pair : (gj + 1) * s.sub_j // pair,
                    gi * s.sub_i * pair : (gi + 1) * s.sub_i * pair,
                    :,
                ] = y.reshape(s.sub_j // pair, s.sub_i * pair, cols)
        pl.when(u + 2 < s.loads)(lambda: x_copy(u + 2).start())

    def send_amplitudes(n):
        each_peer(lambda to: a_copy(n, to).start())
        pltpu.make_async_copy(outgoing(n, me), place(n, me), a_recv_sem.at[n]).start()

    def dress(n):
        span = min(512, CORES * cols)
        for at in range(0, CORES * cols, span):
            kept = mask[:, at : at + span]
            masked = slab[n, :, at : at + span] * kept
            mixed = dot(mix[...], masked)
            dressed = (masked.astype(F32) + mixed).astype(BF16)
            tau[:, at : at + span] = dressed * kept

    def in_turn(k):
        return jnp.where(z * 2 < depth, last - k, k)

    tiles_copy = pltpu.make_async_copy(tiles_hbm, tiles_ref, tiles_sem.at[0])
    int_tiles_copy = pltpu.make_async_copy(int_tiles_hbm, int_tiles_ref, tiles_sem.at[1])
    x_copy(0).start()
    tiles_copy.start()
    int_tiles_copy.start()
    barrier = pltpu.get_barrier_semaphore()

    def greet(device):
        pl.semaphore_signal(barrier, inc=1, device_id=device, device_id_type=MESH)

    each_peer(lambda to: greet(at_rank(to)))
    pl.when(z > 0)(lambda: greet(along(z - 1)))
    pl.when(z < last)(lambda: greet(along(z + 1)))
    for k in range(depth):
        int_local(in_turn(k)).start()
    if s.loads > 1:
        x_copy(1).start()

    r, c = iota((s.count, 1), 0), iota((1, s.count), 1)
    natural = ((r // pair) % s.sub_i) * s.sub_j + (r // (pair * s.sub_i)) * pair + r % pair
    split_rows[...] = one_hot(c == natural)
    prepare(0)
    tiles_copy.wait()
    int_tiles_copy.wait()
    kept_tiles = tiles_ref[...].astype(F32)
    kept_tiles = jnp.concatenate(
        [kept_tiles, jnp.zeros((kept_tiles.shape[0], TILE - s.firsts), F32)], axis=1
    )
    kept_tiles = jnp.concatenate(
        [kept_tiles, jnp.zeros((TILE - kept_tiles.shape[0], TILE), F32)], axis=0
    )
    map_send[...] = kept_tiles.T[: s.firsts]
    own_tiles = cols // TILE
    if pack:
        int_tiles = int_tiles_ref[...].astype(F32)
        int_map[aligned(core * own_tiles, own_tiles), :] = jnp.concatenate(
            [int_tiles, jnp.zeros((own_tiles, TILE - int_tiles.shape[1]), F32)], axis=1
        )

    def mask_ints(k):
        d = in_turn(k)
        int_local(d).wait()
        tiles = int_tiles_ref.shape[1]
        spread = one_hot(
            iota((1, s.width), 1) // TILE == iota((tiles, 1), 0) - d * s.tiles
        )
        kept = dot(int_tiles_ref[...].astype(F32).astype(BF16), spread).astype(BF16)
        for j in range(own_tiles):
            span = aligned(core * cols + j * TILE, TILE)
            ints[d, span, :] = ints[d, span, :] * kept[j : j + 1, :]

    mask_ints(0)

    ends = jnp.where(z > 0, 1, 0) + jnp.where(z < last, 1, 0)
    pl.semaphore_wait(barrier, group - 1 + ends)

    each_peer(lambda to: map_copy(to, me).start())
    own_map = pltpu.make_async_copy(map_send, map_place(me), map_recv_sem.at[me])
    own_map.start()
    if pack:

        def int_map_copy(source):
            span = aligned(source * own_tiles, own_tiles)
            mine = aligned(core * own_tiles, own_tiles)
            return remote(
                int_map.at[mine],
                int_map.at[span],
                int_map_send_sem,
                int_map_recv_sem,
                at_rank(b * CORES + 1 - core),
            )

        int_map_copy(core).start()
    send_amplitudes(0)

    int_copy(in_turn(0), core).start()

    def mask_more(k, carry):
        mask_ints(k)
        int_copy(in_turn(k), core).start()
        return carry

    lax.fori_loop(1, depth, mask_more, 0)
    for n in range(1, min(AHEAD + 1, chunks)):
        if n % s.per_load == 0:
            prepare(n // s.per_load)
        if n < AHEAD:
            send_amplitudes(n)
    tall = one_hot(iota((s.rows, s.occ), 0) // pair == iota((s.rows, s.occ), 1))
    if pair == 1:
        mix[...] = occ_ref[...]
    else:
        wide = one_hot(iota((s.occ, s.rows), 1) // pair == iota((s.occ, s.rows), 0))
        stretched = dot(dot(tall, occ_ref[...]).astype(BF16), wide)
        same = iota((s.rows, s.rows), 0) % pair == iota((s.rows, s.rows), 1) % pair
        mix[...] = jnp.where(same, stretched, 0.0).astype(BF16)

    own_map.wait()
    each_peer(lambda source: map_copy(source, source).wait_recv())
    tiles_all = dot(tall, map_recv[...].astype(BF16)).astype(BF16)
    lane = iota((CORES * TILE, 1), 0)
    col = iota((1, CORES * cols), 1)
    mask[...] = dot(
        tiles_all, one_hot(lane == (col // cols) * TILE + (col % cols) // TILE)
    ).astype(BF16)

    if pack:
        others = (depth - 1) * s.tiles
        room = s.room

        def spot_copy(src, sem, dst, recv, device):
            return remote(src, dst, sem, recv, device)

        def right_spot(src):
            return remote(
                src, right_spots, spot_send_sem.at[0], right_spot_sem, along((z + 1) % depth)
            )

        def left_spot(src):
            return remote(
                src, left_spots, spot_send_sem.at[1], left_spot_sem, along((z + last) % depth)
            )

        int_map_copy(1 - core).wait_recv()

        @pl.when((z == 0) | (z == last))
        def _():
            hits = jnp.zeros((s.occ, TILE), F32)
            for k in range(CORES):
                rows = int_map[k * own_tiles : (k + 1) * own_tiles, :]
                rows = jnp.concatenate([rows, jnp.zeros((TILE - own_tiles, TILE), F32)], axis=0)
                hits += dot(
                    map_recv[:, k * TILE : (k + 1) * TILE].astype(BF16), rows.astype(BF16)
                )
            hits = jnp.where(hits > 0.5, 1.0, 0.0).T
            hits = jnp.where(z == 0, hits[s.tiles : s.tiles + others], hits[:others])
            hits = jnp.concatenate([hits, jnp.zeros((LEAST - others, TILE), F32)], axis=0)
            marks = hits.astype(BF16)
            i, k = iota((TILE, TILE), 0), iota((TILE, TILE), 1)
            ahead = dot(marks, one_hot(i < k))
            totals = dot(marks, jnp.ones((TILE, TILE), BF16))
            r, c = iota((LEAST, LEAST), 0), iota((LEAST, LEAST), 1)
            before = jnp.where(z == 0, one_hot(c > r), one_hot(c < r))
            ahead += dot(before, totals.astype(BF16))
            spots[0:LEAST, :] = jnp.where(hits > 0.5, ahead, -1.0)
            total = jnp.sum(hits, axis=0, keepdims=True)
            total = jnp.sum(total, axis=1, keepdims=True)
            spots[LEAST:, :] = jnp.broadcast_to(total, (spots.shape[0] - LEAST, TILE))
            pl.when(z == 0)(lambda: right_spot(spots).start())
            pl.when(z == last)(lambda: left_spot(spots).start())
            at = iota((room, TILE), 0).astype(F32)
            for k in range(others):
                choose[0:room, k * TILE : (k + 1) * TILE] = one_hot(at == spots[k : k + 1, :])

        def restore(ref):
            where = jnp.concatenate(
                [ref[0:LEAST, :], jnp.full((TILE - LEAST, TILE), -1.0, F32)], axis=0
            ).T
            at = iota((TILE, room), 1).astype(F32)
            for k in range(others):
                choose[k * TILE : (k + 1) * TILE, 0:room] = one_hot(at == where[:, k : k + 1])

        @pl.when(z == 1)
        def _():
            right_spot(spots).wait_recv()
            right_spot(right_spots).start()

        @pl.when(z == last - 1)
        def _():
            left_spot(spots).wait_recv()
            left_spot(left_spots).start()

        pieces = []
        for begin in range(0, room, piece):
            pieces.append((begin, min(room, begin + piece)))

        def packed_copy(n, o, to_right):
            begin, end = pieces[o]
            base = 2 * flat if to_right else 0
            return remote(
                packed.at[n % 2, pl.ds(begin, end - begin), :],
                inbox_rows(n, base + begin, end - begin),
                z_send_sem.at[n, o],
                (right_sem if to_right else left_sem).at[n, o],
                along((z + 1) % depth) if to_right else along((z + last) % depth),
            )

        def inbox_rows(n, begin, size):
            slot = begin // flat
            return inbox.at[n, slot, pl.ds(begin - slot * flat, size), :]

        def packed_left(n):
            for o in range(len(pieces)):
                packed_copy(n, o, True).wait_send()


    farther = jnp.maximum(z, last - z)
    dense_right = (z > 0) if not pack else (z > 1)
    dense_left = (z < last) if not pack else (z < last - 1)

    def add_into(n, d, slot, h):
        rows = slice(h * piece, (h + 1) * piece)
        total = part[n, d, rows, :].astype(F32) + inbox[n, slot, rows, :].astype(F32)
        part[n, d, rows, :] = total.astype(BF16)

    def ladder_step(t):
        a_arrived(t).wait()
        pl.when(t + AHEAD < chunks)(lambda: send_amplitudes(t + AHEAD))
        dress(t)

        def ladder(k, carry):
            d = in_turn(k)
            pl.when(t == 0)(lambda: int_copy(d, 1 - core).wait_recv())
            y = dot(tau[...], ints[d]).astype(BF16)
            for k in range(s.tiles):
                part[t, d, k * s.rows : (k + 1) * s.rows, :] = y[:, k * TILE : (k + 1) * TILE]
            if not pack:
                for h in range(PARTS):
                    pl.when((z == 0) & (d > 0))(lambda: right_copy(t, d, PARTS - 1 - h).start())
                    pl.when((z == last) & (d < last))(lambda: left_copy(t, d, h).start())
            return carry

        lax.fori_loop(0, depth, ladder, 0)
        if pack:

            @pl.when((z == 0) | (z == last))
            def _():
                pl.when(t >= 2)(lambda: packed_left(t - 2))
                first = jnp.where(z == 0, 1, 0)
                x = part[t, pl.ds(first, depth - 1)].reshape(s.sent, TILE)
                for o, (begin, end) in enumerate(pieces):
                    if begin % flat == 0:
                        until = min(room, begin + flat)
                        packed[t % 2, begin:until, :] = dot(choose[begin:until, :], x).astype(BF16)
                    pl.when(z == 0)(lambda: packed_copy(t, o, True).start())
                    pl.when(z == last)(lambda: packed_copy(t, o, False).start())

        a_left(t).wait()

        @pl.when(t == 0)
        def _():
            for at in range(0, turned.shape[1], 512):
                turned[:, at : at + 512] = jnp.zeros((half, 512), BF16)
            if pack:
                pl.when(z == 1)(lambda: restore(right_spots))
                pl.when(z == last - 1)(lambda: restore(left_spots))

        ready = t + AHEAD + 1
        pl.when((ready < chunks) & (ready % s.per_load == 0))(
            lambda: prepare(ready // s.per_load)
        )

    def unpack_step(m, to_right):
        base = 2 if to_right else 0
        count = (depth - 1) * PARTS
        x = []
        for o in range(count):
            if o < len(pieces):
                packed_copy(m, o, to_right).wait_recv()
                begin, end = pieces[o]
                rows = slice(begin % flat, begin % flat + end - begin)
                x.append(inbox[m, base + begin // flat, rows, :])
            g = count - 1 - o if to_right else o
            d, h = g // PARTS + (1 if to_right else 0), g % PARTS
            y = dot(choose[g * piece : (g + 1) * piece, :end], jnp.concatenate(x, axis=0))
            rows = slice(h * piece, (h + 1) * piece)
            part[m, d, rows, :] = (part[m, d, rows, :].astype(F32) + y).astype(BF16)
            if to_right and d > 1:
                right_copy(m, d, h).start()
            if not to_right and d < depth - 2:
                left_copy(m, d, h).start()

    def right_step(m):
        def pass_on(k, carry):
            d = last - k
            for h in reversed(range(PARTS)):
                right_copy(m, d, h).wait_recv()
                add_into(m, d, d + 1, h)
                right_copy(m, d, h).start()
            return carry

        lax.fori_loop(0, last - z, pass_on, 0)

    def left_step(m):
        def pass_on(d, carry):
            for h in range(PARTS):
                left_copy(m, d, h).wait_recv()
                add_into(m, d, d, h)
                left_copy(m, d, h).start()
            return carry

        lax.fori_loop(0, z, pass_on, 0)

    def last_step(m):
        acc[...] = part[m, z].astype(F32)

        @pl.when(dense_right)
        def _():
            for h in range(PARTS):
                right_copy(m, z, h).wait_recv()
            acc[...] += inbox[m, z + 1].astype(F32)

        @pl.when(dense_left)
        def _():
            for h in range(PARTS):
                left_copy(m, z, h).wait_recv()
            acc[...] += inbox[m, z].astype(F32)

        for k in range(s.tiles):
            c_send[m, :, k * TILE : (k + 1) * TILE] = acc[k * s.rows : (k + 1) * s.rows, :].astype(
                BF16
            )
        each_peer(lambda to: c_copy(m, to).start())
        c_own(m).start()

    def turn_step(u):
        span = s.sub_i * s.occ
        r = iota((s.count, 1), 0)
        spot = ((r // pair) % s.sub_i) * s.occ + (r // (pair * s.sub_i)) * pair + r % pair
        per = s.sub_j // pair
        for gj in range(s.load // s.sub_j):
            shift = u * s.load + gj * s.sub_j
            chosen[...] = one_hot(iota((1, span), 1) - shift == spot)
            if gj == 0:
                for k in range(s.per_load):
                    c_arrived(u * s.per_load + k).wait()
            for gi in range(s.firsts // s.sub_i):
                pieces = []
                begin = gj * per
                while begin < (gj + 1) * per:
                    end = min((gj + 1) * per, (begin // group + 1) * group)
                    k = begin // group
                    pieces.append(
                        c_recv[
                            u * s.per_load + k,
                            begin - k * group : end - k * group,
                            gi * s.sub_i * pair : (gi + 1) * s.sub_i * pair,
                            :,
                        ]
                    )
                    begin = end
                x = jnp.concatenate(pieces, axis=0) if len(pieces) > 1 else pieces[0]
                x = x.reshape(s.count, half).T
                step = min(512, span)
                for at in range(0, span, step):
                    y = dot(x, chosen[:, at : at + step]).astype(BF16)
                    cols_at = gi * span + at
                    turned[:, cols_at : cols_at + step] = turned[:, cols_at : cols_at + step] + y

    dense_sender = (z > 0) & (z < last) if pack else z == z

    def finish(n, carry):
        def sent(d, carry):
            for h in range(PARTS):
                pl.when((d != z) & dense_sender)(lambda: right_copy(n, d, h).wait_send())
            return carry

        lax.fori_loop(0, depth, sent, 0)
        c_left(n).wait()
        return carry

    def finish_start():
        each_peer(lambda to: map_copy(to, me).wait_send())
        for d in range(depth):
            int_copy(d, core).wait_send()

    def step(t, carry):
        pl.when(t < chunks)(lambda: ladder_step(t))

        m = t - z
        live = (m >= 0) & (m < chunks)
        m_left = t - (last - z)
        live_left = (m_left >= 0) & (m_left < chunks)
        m_last = t - farther
        m_out = m_last - 1
        whole = (m_out >= 0) & (m_out < chunks) & (m_out % s.per_load == s.per_load - 1)

        def unpack(when):
            pl.when((z == 1) & live & when)(lambda: unpack_step(m, True))
            pl.when((z == last - 1) & live_left & when)(lambda: unpack_step(m_left, False))

        if pack:
            unpack(t < chunks)
        pl.when(dense_right & live)(lambda: right_step(m))
        pl.when(dense_left & live_left)(lambda: left_step(m_left))
        pl.when((m_last >= 0) & (m_last < chunks))(lambda: last_step(m_last))
        if pack:
            unpack(t >= chunks)
        pl.when(whole)(lambda: turn_step(m_out // s.per_load))
        pl.when(t == 1)(finish_start)

        @pl.when((t >= LATE) & (t - LATE < chunks))
        def _():
            finish(t - LATE, 0)


        return carry

    lax.fori_loop(0, chunks + depth, step, 0)

    if pack:

        @pl.when(z > 1)
        def _():
            right_spot(spots).wait_recv()
            pl.when(z < last)(lambda: right_spot(right_spots).start())

        @pl.when(z < last - 1)
        def _():
            left_spot(spots).wait_recv()
            pl.when(z > 0)(lambda: left_spot(left_spots).start())

        pl.when(z < last)(lambda: right_spot(spots).wait_send())
        pl.when(z > 0)(lambda: left_spot(spots).wait_send())
        rows = slice(LEAST, LEAST + 8)
        from_left = jnp.where(z == 0, spots[rows, :], right_spots[rows, :])
        from_right = jnp.where(z == last, spots[rows, :], left_spots[rows, :])
        flag_ref[0, 0] = jnp.max(jnp.maximum(from_left, from_right))
        int_map_copy(core).wait_send()

        @pl.when((z == 0) | (z == last))
        def _():
            for n in range(max(0, chunks - 2), chunks):
                packed_left(n)

    else:
        flag_ref[0, 0] = jnp.float32(0)

    lax.fori_loop(max(0, chunks + depth - LATE), chunks, finish, 0)


def residual(s, pack, amplitudes, amp_tiles, occ_coupling, integrals, int_tiles):
    vmem, dma = pltpu.VMEM, pltpu.SemaphoreType.DMA
    any_space = pl.BlockSpec(memory_space=pl.ANY)
    in_vmem = pl.BlockSpec(memory_space=pltpu.VMEM)
    chunks, depth, group = s.chunks, s.depth, s.group
    both = CORES * s.cols
    scratch = [
        vmem((2, s.firsts, s.load, s.cols), BF16),
        vmem((s.slots, s.per_load * group, s.block, s.cols), BF16),
        vmem((chunks, s.rows, both), BF16),
        vmem((s.rows, both), BF16),
        vmem((s.rows, both), BF16),
        vmem(amp_tiles.shape[::-1], jnp.int32),
        vmem(int_tiles.shape, jnp.int32),
        vmem((s.firsts, TILE), F32),
        vmem((s.occ, CORES * TILE), F32),
        vmem((depth, both, s.width), BF16),
        vmem((chunks, depth, s.flat, TILE), BF16),
        vmem((chunks, depth + 1, s.flat, TILE), BF16),
        vmem((s.flat, TILE), F32),
        vmem((chunks, s.rows, s.width), BF16),
        vmem((chunks, group, s.block, s.half), BF16),
        vmem((s.count, s.count), BF16),
        vmem((s.count, s.sub_i * s.occ), BF16),
        vmem((s.rows, s.rows), BF16),
        dma((2,)),
        dma((2,)),
        dma((chunks,)),
        dma((chunks,)),
        dma((group,)),
        dma((group,)),
        dma((depth,)),
        dma((depth,)),
        dma((depth,)),
        dma((chunks, depth * PARTS)),
        dma((chunks, depth * PARTS)),
        dma((chunks, depth * PARTS)),
        dma((chunks,)),
        dma((chunks,)),
    ]
    if pack:
        scratch += [
            vmem((s.sent, s.sent), BF16),
            vmem((2, s.room, TILE), BF16),
            vmem((LEAST + 8, TILE), F32),
            vmem((LEAST + 8, TILE), F32),
            vmem((LEAST + 8, TILE), F32),
            vmem((CORES * (s.cols // TILE), TILE), F32),
            dma((2,)),
            dma(()),
            dma(()),
            dma(()),
            dma(()),
        ]
    return pl.pallas_call(
        functools.partial(residual_kernel, s, pack),
        out_shape=(
            pltpu.VMEM((s.half, s.firsts * s.occ), BF16),
            jax.ShapeDtypeStruct((1, 1), F32),
        ),
        in_specs=[any_space, any_space, in_vmem, any_space, any_space],
        out_specs=(in_vmem, pl.BlockSpec(memory_space=pltpu.SMEM)),
        scratch_shapes=scratch,
        compiler_params=pltpu.CompilerParams(
            collective_id=1 if pack else 0,
            has_side_effects=True,
            vmem_limit_bytes=58 * 1024 * 1024,
        ),
        name="packed" if pack else "dense",
    )(
        amplitudes.reshape(s.firsts, s.occ, s.cols),
        amp_tiles.T,
        occ_coupling,
        integrals,
        int_tiles,
    )


def shards(mesh_shape, *arrays):
    s = Sizes(mesh_shape, arrays[0], arrays[2], arrays[3])
    if PACK and s.can_pack:
        out, used = residual(s, True, *arrays)
        return lax.cond(
            used[0, 0] > s.room, lambda: residual(s, False, *arrays)[0], lambda: out
        )
    return residual(s, False, *arrays)[0]


PACK = True


def solution(mesh):
    shape = mesh.devices.shape
    in_specs = (P("bulk", "cuts"), P("bulk", "cuts"), P(), P("cuts", None), P("cuts", None))
    return jax.shard_map(
        functools.partial(shards, shape),
        mesh=mesh,
        in_specs=in_specs,
        out_specs=P("cuts", "bulk"),
        check_vma=False,
    )
```

```python
import functools

import jax
import jax.numpy as jnp
from jax import lax
from jax.experimental import pallas as pl
from jax.experimental.pallas import tpu as pltpu
from jax.sharding import PartitionSpec as P

TILE = 128
CORES = 2
LEAST = 16
BLOCK = 256
AHEAD = 2
LATE = 5
PARTS = 1
MESH = pl.DeviceIdType.MESH
F32 = jnp.float32
BF16 = jnp.bfloat16


def dot(a, b):
    return jnp.dot(a, b, preferred_element_type=F32)


def iota(shape, axis):
    return lax.broadcasted_iota(jnp.int32, shape, axis)


def one_hot(condition):
    return jnp.where(condition, 1.0, 0.0).astype(BF16)


class Sizes:
    def __init__(self, mesh_shape, amplitudes, occ_coupling, integrals):
        self.bulk, cuts = mesh_shape
        self.depth = cuts // CORES
        self.group = self.bulk * CORES
        local_rows, self.cols = amplitudes.shape
        self.occ = occ_coupling.shape[0]
        self.firsts = local_rows // self.occ
        self.pair = max(1, LEAST // self.firsts)
        self.seconds = self.pair * self.group
        self.chunks = self.occ // self.seconds
        self.load = max(LEAST, self.seconds)
        self.per_load = self.load // self.seconds
        self.loads = self.occ // self.load
        self.slots = 3 if self.per_load > 1 else AHEAD + 2
        self.width = integrals.shape[1] // self.depth
        self.half = self.width // CORES
        self.rows = self.pair * self.occ
        self.block = self.firsts * self.pair
        self.sub_j = min(self.load, max(LEAST, BLOCK // self.firsts))
        self.sub_i = min(self.firsts, BLOCK // self.sub_j)
        self.count = self.sub_i * self.sub_j
        self.tiles = self.width // TILE
        self.flat = self.tiles * self.rows
        self.piece = self.flat // PARTS
        self.sent = (self.depth - 1) * self.flat
        self.can_pack = self.pair == 1 and self.depth == 4 and self.occ == TILE
        self.room = self.sent * 26 // 32 // LEAST * LEAST


def residual_kernel(s, pack, *refs):
    (
        amp_hbm,
        tiles_hbm,
        occ_ref,
        int_hbm,
        int_tiles_hbm,
        turned,
        flag_ref,
        x_buf,
        send_buf,
        slab,
        tau,
        mask,
        tiles_ref,
        int_tiles_ref,
        map_send,
        map_recv,
        ints,
        part,
        inbox,
        acc,
        c_send,
        c_recv,
        split_rows,
        chosen,
        mix,
        x_sem,
        tiles_sem,
        a_send_sem,
        a_recv_sem,
        map_send_sem,
        map_recv_sem,
        int_local_sem,
        int_send_sem,
        int_recv_sem,
        z_send_sem,
        right_sem,
        left_sem,
        c_send_sem,
        c_recv_sem,
    ) = refs[:39]
    if pack:
        (
            choose,
            packed,
            spots,
            right_spots,
            left_spots,
            int_map,
            spot_send_sem,
            right_spot_sem,
            left_spot_sem,
            int_map_send_sem,
            int_map_recv_sem,
        ) = refs[39:]
    depth, group, chunks, cols, pair = s.depth, s.group, s.chunks, s.cols, s.pair
    block, half, flat, piece = s.block, s.half, s.flat, s.piece
    b = lax.axis_index("bulk")
    cut = lax.axis_index("cuts")
    z = cut // CORES
    core = cut % CORES
    me = b * CORES + core
    last = depth - 1

    def aligned(start, size):
        return pl.ds(pl.multiple_of(start, size), size)

    def at_rank(rank):
        return (rank // CORES, z * CORES + rank % CORES)

    def along(zz):
        return (b, zz * CORES + core)

    def remote(src, dst, send_sem, recv_sem, device):
        return pltpu.make_async_remote_copy(
            src_ref=src,
            dst_ref=dst,
            send_sem=send_sem,
            recv_sem=recv_sem,
            device_id=device,
            device_id_type=MESH,
        )

    def each_peer(body):
        def step(k, carry):
            body((me + k) % group)
            return carry

        lax.fori_loop(1, group, step, 0)

    def x_copy(u):
        return pltpu.make_async_copy(
            amp_hbm.at[:, aligned(u * s.load, s.load), :], x_buf.at[u % 2], x_sem.at[u % 2]
        )

    def place(n, rank):
        return slab.at[n, aligned((rank // CORES) * block, block), aligned((rank % CORES) * cols, cols)]

    def outgoing(n, to):
        return send_buf.at[(n // s.per_load) % s.slots, (n % s.per_load) * group + to]

    def a_copy(n, to):
        return remote(
            outgoing(n, to), place(n, me), a_send_sem.at[n], a_recv_sem.at[n], at_rank(to)
        )

    def a_arrived(n):
        return pltpu.make_async_copy(slab.at[n], slab.at[n], a_recv_sem.at[n])

    def a_left(n):
        ref = send_buf.at[(n // s.per_load) % s.slots, pl.ds((n % s.per_load) * group, group - 1)]
        return pltpu.make_async_copy(ref, ref, a_send_sem.at[n])

    def map_place(source):
        return map_recv.at[
            aligned((source // CORES) * s.firsts, s.firsts), aligned((source % CORES) * TILE, TILE)
        ]

    def map_copy(to, source):
        return remote(
            map_send, map_place(source), map_send_sem.at[to], map_recv_sem.at[source], at_rank(to)
        )

    def int_local(d):
        return pltpu.make_async_copy(
            int_hbm.at[:, aligned(d * s.width, s.width)],
            ints.at[d, aligned(core * cols, cols), :],
            int_local_sem.at[d],
        )

    def int_copy(d, source):
        return remote(
            ints.at[d, aligned(core * cols, cols), :],
            ints.at[d, aligned(source * cols, cols), :],
            int_send_sem.at[d],
            int_recv_sem.at[d],
            at_rank(b * CORES + 1 - core),
        )

    def right_copy(n, d, h):
        span = pl.ds(h * piece, piece)
        return remote(
            part.at[n, d, span],
            inbox.at[n, d + 1, span],
            z_send_sem.at[n, d * PARTS + h],
            right_sem.at[n, d * PARTS + h],
            along((z + 1) % depth),
        )

    def left_copy(n, d, h):
        span = pl.ds(h * piece, piece)
        return remote(
            part.at[n, d, span],
            inbox.at[n, d, span],
            z_send_sem.at[n, d * PARTS + h],
            left_sem.at[n, d * PARTS + h],
            along((z + last) % depth),
        )

    def c_copy(n, to):
        return remote(
            c_send.at[n, aligned((to // CORES) * block, block), aligned((to % CORES) * half, half)],
            c_recv.at[n, me],
            c_send_sem.at[n],
            c_recv_sem.at[n],
            at_rank(to),
        )

    def c_own(n):
        return pltpu.make_async_copy(
            c_send.at[n, aligned(b * block, block), aligned(core * half, half)],
            c_recv.at[n, me],
            c_recv_sem.at[n],
        )

    def c_arrived(n):
        return pltpu.make_async_copy(c_recv.at[n], c_recv.at[n], c_recv_sem.at[n])

    def c_left(n):
        ref = c_recv.at[n, pl.ds(0, group - 1)]
        return pltpu.make_async_copy(ref, ref, c_send_sem.at[n])

    def prepare(u):
        x_copy(u).wait()
        for gi in range(s.firsts // s.sub_i):
            for gj in range(s.load // s.sub_j):
                x = x_buf[
                    u % 2,
                    gi * s.sub_i : (gi + 1) * s.sub_i,
                    gj * s.sub_j : (gj + 1) * s.sub_j,
                    :,
                ]
                y = dot(split_rows[...], x.reshape(s.count, cols)).astype(BF16)
                send_buf[
                    u % s.slots,
                    gj * s.sub_j // pair : (gj + 1) * s.sub_j // pair,
                    gi * s.sub_i * pair : (gi + 1) * s.sub_i * pair,
                    :,
                ] = y.reshape(s.sub_j // pair, s.sub_i * pair, cols)
        pl.when(u + 2 < s.loads)(lambda: x_copy(u + 2).start())

    def send_amplitudes(n):
        each_peer(lambda to: a_copy(n, to).start())
        pltpu.make_async_copy(outgoing(n, me), place(n, me), a_recv_sem.at[n]).start()

    def dress(n):
        span = min(512, CORES * cols)
        for at in range(0, CORES * cols, span):
            kept = mask[:, at : at + span]
            masked = slab[n, :, at : at + span] * kept
            mixed = dot(mix[...], masked)
            dressed = (masked.astype(F32) + mixed).astype(BF16)
            tau[:, at : at + span] = dressed * kept

    def in_turn(k):
        return jnp.where(z * 2 < depth, last - k, k)

    tiles_copy = pltpu.make_async_copy(tiles_hbm, tiles_ref, tiles_sem.at[0])
    int_tiles_copy = pltpu.make_async_copy(int_tiles_hbm, int_tiles_ref, tiles_sem.at[1])
    x_copy(0).start()
    tiles_copy.start()
    int_tiles_copy.start()
    barrier = pltpu.get_barrier_semaphore()

    def greet(device):
        pl.semaphore_signal(barrier, inc=1, device_id=device, device_id_type=MESH)

    each_peer(lambda to: greet(at_rank(to)))
    pl.when(z > 0)(lambda: greet(along(z - 1)))
    pl.when(z < last)(lambda: greet(along(z + 1)))
    for k in range(depth):
        int_local(in_turn(k)).start()
    if s.loads > 1:
        x_copy(1).start()

    r, c = iota((s.count, 1), 0), iota((1, s.count), 1)
    natural = ((r // pair) % s.sub_i) * s.sub_j + (r // (pair * s.sub_i)) * pair + r % pair
    split_rows[...] = one_hot(c == natural)
    prepare(0)
    tiles_copy.wait()
    int_tiles_copy.wait()
    kept_tiles = tiles_ref[...].astype(F32)
    kept_tiles = jnp.concatenate(
        [kept_tiles, jnp.zeros((kept_tiles.shape[0], TILE - s.firsts), F32)], axis=1
    )
    kept_tiles = jnp.concatenate(
        [kept_tiles, jnp.zeros((TILE - kept_tiles.shape[0], TILE), F32)], axis=0
    )
    map_send[...] = kept_tiles.T[: s.firsts]
    own_tiles = cols // TILE
    if pack:
        int_tiles = int_tiles_ref[...].astype(F32)
        int_map[aligned(core * own_tiles, own_tiles), :] = jnp.concatenate(
            [int_tiles, jnp.zeros((own_tiles, TILE - int_tiles.shape[1]), F32)], axis=1
        )

    def mask_ints(k):
        d = in_turn(k)
        int_local(d).wait()
        tiles = int_tiles_ref.shape[1]
        spread = one_hot(
            iota((1, s.width), 1) // TILE == iota((tiles, 1), 0) - d * s.tiles
        )
        kept = dot(int_tiles_ref[...].astype(F32).astype(BF16), spread).astype(BF16)
        for j in range(own_tiles):
            span = aligned(core * cols + j * TILE, TILE)
            ints[d, span, :] = ints[d, span, :] * kept[j : j + 1, :]

    mask_ints(0)

    ends = jnp.where(z > 0, 1, 0) + jnp.where(z < last, 1, 0)
    pl.semaphore_wait(barrier, group - 1 + ends)

    each_peer(lambda to: map_copy(to, me).start())
    own_map = pltpu.make_async_copy(map_send, map_place(me), map_recv_sem.at[me])
    own_map.start()
    if pack:

        def int_map_copy(source):
            span = aligned(source * own_tiles, own_tiles)
            mine = aligned(core * own_tiles, own_tiles)
            return remote(
                int_map.at[mine],
                int_map.at[span],
                int_map_send_sem,
                int_map_recv_sem,
                at_rank(b * CORES + 1 - core),
            )

        int_map_copy(core).start()
    send_amplitudes(0)

    int_copy(in_turn(0), core).start()

    def mask_more(k, carry):
        mask_ints(k)
        int_copy(in_turn(k), core).start()
        return carry

    lax.fori_loop(1, depth, mask_more, 0)
    for n in range(1, min(AHEAD + 1, chunks)):
        if n % s.per_load == 0:
            prepare(n // s.per_load)
        if n < AHEAD:
            send_amplitudes(n)
    tall = one_hot(iota((s.rows, s.occ), 0) // pair == iota((s.rows, s.occ), 1))
    if pair == 1:
        mix[...] = occ_ref[...]
    else:
        wide = one_hot(iota((s.occ, s.rows), 1) // pair == iota((s.occ, s.rows), 0))
        stretched = dot(dot(tall, occ_ref[...]).astype(BF16), wide)
        same = iota((s.rows, s.rows), 0) % pair == iota((s.rows, s.rows), 1) % pair
        mix[...] = jnp.where(same, stretched, 0.0).astype(BF16)

    own_map.wait()
    each_peer(lambda source: map_copy(source, source).wait_recv())
    tiles_all = dot(tall, map_recv[...].astype(BF16)).astype(BF16)
    lane = iota((CORES * TILE, 1), 0)
    col = iota((1, CORES * cols), 1)
    mask[...] = dot(
        tiles_all, one_hot(lane == (col // cols) * TILE + (col % cols) // TILE)
    ).astype(BF16)

    if pack:
        others = (depth - 1) * s.tiles
        room = s.room

        def spot_copy(src, sem, dst, recv, device):
            return remote(src, dst, sem, recv, device)

        def right_spot(src):
            return remote(
                src, right_spots, spot_send_sem.at[0], right_spot_sem, along((z + 1) % depth)
            )

        def left_spot(src):
            return remote(
                src, left_spots, spot_send_sem.at[1], left_spot_sem, along((z + last) % depth)
            )

        int_map_copy(1 - core).wait_recv()

        @pl.when((z == 0) | (z == last))
        def _():
            hits = jnp.zeros((s.occ, TILE), F32)
            for k in range(CORES):
                rows = int_map[k * own_tiles : (k + 1) * own_tiles, :]
                rows = jnp.concatenate([rows, jnp.zeros((TILE - own_tiles, TILE), F32)], axis=0)
                hits += dot(
                    map_recv[:, k * TILE : (k + 1) * TILE].astype(BF16), rows.astype(BF16)
                )
            hits = jnp.where(hits > 0.5, 1.0, 0.0).T
            hits = jnp.where(z == 0, hits[s.tiles : s.tiles + others], hits[:others])
            hits = jnp.concatenate([hits, jnp.zeros((LEAST - others, TILE), F32)], axis=0)
            marks = hits.astype(BF16)
            i, k = iota((TILE, TILE), 0), iota((TILE, TILE), 1)
            ahead = dot(marks, one_hot(i < k))
            totals = dot(marks, jnp.ones((TILE, TILE), BF16))
            r, c = iota((LEAST, LEAST), 0), iota((LEAST, LEAST), 1)
            before = jnp.where(z == 0, one_hot(c > r), one_hot(c < r))
            ahead += dot(before, totals.astype(BF16))
            spots[0:LEAST, :] = jnp.where(hits > 0.5, ahead, -1.0)
            total = jnp.sum(hits, axis=0, keepdims=True)
            total = jnp.sum(total, axis=1, keepdims=True)
            spots[LEAST:, :] = jnp.broadcast_to(total, (spots.shape[0] - LEAST, TILE))
            pl.when(z == 0)(lambda: right_spot(spots).start())
            pl.when(z == last)(lambda: left_spot(spots).start())
            at = iota((room, TILE), 0).astype(F32)
            for k in range(others):
                choose[0:room, k * TILE : (k + 1) * TILE] = one_hot(at == spots[k : k + 1, :])

        def restore(ref):
            where = jnp.concatenate(
                [ref[0:LEAST, :], jnp.full((TILE - LEAST, TILE), -1.0, F32)], axis=0
            ).T
            at = iota((TILE, room), 1).astype(F32)
            for k in range(others):
                choose[k * TILE : (k + 1) * TILE, 0:room] = one_hot(at == where[:, k : k + 1])

        @pl.when(z == 1)
        def _():
            right_spot(spots).wait_recv()
            right_spot(right_spots).start()

        @pl.when(z == last - 1)
        def _():
            left_spot(spots).wait_recv()
            left_spot(left_spots).start()

        pieces = []
        for begin in range(0, room, piece):
            pieces.append((begin, min(room, begin + piece)))

        def packed_copy(n, o, to_right):
            begin, end = pieces[o]
            base = 2 * flat if to_right else 0
            return remote(
                packed.at[n % 2, pl.ds(begin, end - begin), :],
                inbox_rows(n, base + begin, end - begin),
                z_send_sem.at[n, o],
                (right_sem if to_right else left_sem).at[n, o],
                along((z + 1) % depth) if to_right else along((z + last) % depth),
            )

        def inbox_rows(n, begin, size):
            slot = begin // flat
            return inbox.at[n, slot, pl.ds(begin - slot * flat, size), :]

        def packed_left(n):
            for o in range(len(pieces)):
                packed_copy(n, o, True).wait_send()


    farther = jnp.maximum(z, last - z)
    dense_right = (z > 0) if not pack else (z > 1)
    dense_left = (z < last) if not pack else (z < last - 1)

    def add_into(n, d, slot, h):
        rows = slice(h * piece, (h + 1) * piece)
        total = part[n, d, rows, :].astype(F32) + inbox[n, slot, rows, :].astype(F32)
        part[n, d, rows, :] = total.astype(BF16)

    def ladder_step(t):
        a_arrived(t).wait()
        pl.when(t + AHEAD < chunks)(lambda: send_amplitudes(t + AHEAD))
        dress(t)

        def ladder(k, carry):
            d = in_turn(k)
            pl.when(t == 0)(lambda: int_copy(d, 1 - core).wait_recv())
            y = dot(tau[...], ints[d]).astype(BF16)
            for k in range(s.tiles):
                part[t, d, k * s.rows : (k + 1) * s.rows, :] = y[:, k * TILE : (k + 1) * TILE]
            if not pack:
                for h in range(PARTS):
                    pl.when((z == 0) & (d > 0))(lambda: right_copy(t, d, PARTS - 1 - h).start())
                    pl.when((z == last) & (d < last))(lambda: left_copy(t, d, h).start())
            return carry

        lax.fori_loop(0, last, ladder, 0)
        if pack:

            @pl.when((z == 0) | (z == last))
            def _():
                pl.when(t >= 2)(lambda: packed_left(t - 2))
                first = jnp.where(z == 0, 1, 0)
                x = part[t, pl.ds(first, depth - 1)].reshape(s.sent, TILE)
                for o, (begin, end) in enumerate(pieces):
                    if begin % flat == 0:
                        until = min(room, begin + flat)
                        packed[t % 2, begin:until, :] = dot(choose[begin:until, :], x).astype(BF16)
                    pl.when(z == 0)(lambda: packed_copy(t, o, True).start())
                    pl.when(z == last)(lambda: packed_copy(t, o, False).start())

        ladder(last, 0)
        a_left(t).wait()

        @pl.when(t == 0)
        def _():
            for at in range(0, turned.shape[1], 512):
                turned[:, at : at + 512] = jnp.zeros((half, 512), BF16)
            if pack:
                pl.when(z == 1)(lambda: restore(right_spots))
                pl.when(z == last - 1)(lambda: restore(left_spots))

        ready = t + AHEAD + 1
        pl.when((ready < chunks) & (ready % s.per_load == 0))(
            lambda: prepare(ready // s.per_load)
        )

    def unpack_step(m, to_right):
        base = 2 if to_right else 0
        count = (depth - 1) * PARTS
        x = []
        for o in range(count):
            if o < len(pieces):
                packed_copy(m, o, to_right).wait_recv()
                begin, end = pieces[o]
                rows = slice(begin % flat, begin % flat + end - begin)
                x.append(inbox[m, base + begin // flat, rows, :])
            g = count - 1 - o if to_right else o
            d, h = g // PARTS + (1 if to_right else 0), g % PARTS
            y = dot(choose[g * piece : (g + 1) * piece, :end], jnp.concatenate(x, axis=0))
            rows = slice(h * piece, (h + 1) * piece)
            part[m, d, rows, :] = (part[m, d, rows, :].astype(F32) + y).astype(BF16)
            if to_right and d > 1:
                right_copy(m, d, h).start()
            if not to_right and d < depth - 2:
                left_copy(m, d, h).start()

    def right_step(m):
        def pass_on(k, carry):
            d = last - k
            for h in reversed(range(PARTS)):
                right_copy(m, d, h).wait_recv()
                add_into(m, d, d + 1, h)
                right_copy(m, d, h).start()
            return carry

        lax.fori_loop(0, last - z, pass_on, 0)

    def left_step(m):
        def pass_on(d, carry):
            for h in range(PARTS):
                left_copy(m, d, h).wait_recv()
                add_into(m, d, d, h)
                left_copy(m, d, h).start()
            return carry

        lax.fori_loop(0, z, pass_on, 0)

    def last_step(m):
        acc[...] = part[m, z].astype(F32)

        @pl.when(dense_right)
        def _():
            for h in range(PARTS):
                right_copy(m, z, h).wait_recv()
            acc[...] += inbox[m, z + 1].astype(F32)

        @pl.when(dense_left)
        def _():
            for h in range(PARTS):
                left_copy(m, z, h).wait_recv()
            acc[...] += inbox[m, z].astype(F32)

        for k in range(s.tiles):
            c_send[m, :, k * TILE : (k + 1) * TILE] = acc[k * s.rows : (k + 1) * s.rows, :].astype(
                BF16
            )
        each_peer(lambda to: c_copy(m, to).start())
        c_own(m).start()

    def turn_step(u):
        span = s.sub_i * s.occ
        r = iota((s.count, 1), 0)
        spot = ((r // pair) % s.sub_i) * s.occ + (r // (pair * s.sub_i)) * pair + r % pair
        per = s.sub_j // pair
        for gj in range(s.load // s.sub_j):
            shift = u * s.load + gj * s.sub_j
            chosen[...] = one_hot(iota((1, span), 1) - shift == spot)
            if gj == 0:
                for k in range(s.per_load):
                    c_arrived(u * s.per_load + k).wait()
            for gi in range(s.firsts // s.sub_i):
                pieces = []
                begin = gj * per
                while begin < (gj + 1) * per:
                    end = min((gj + 1) * per, (begin // group + 1) * group)
                    k = begin // group
                    pieces.append(
                        c_recv[
                            u * s.per_load + k,
                            begin - k * group : end - k * group,
                            gi * s.sub_i * pair : (gi + 1) * s.sub_i * pair,
                            :,
                        ]
                    )
                    begin = end
                x = jnp.concatenate(pieces, axis=0) if len(pieces) > 1 else pieces[0]
                x = x.reshape(s.count, half).T
                step = min(512, span)
                for at in range(0, span, step):
                    y = dot(x, chosen[:, at : at + step]).astype(BF16)
                    cols_at = gi * span + at
                    turned[:, cols_at : cols_at + step] = turned[:, cols_at : cols_at + step] + y

    dense_sender = (z > 0) & (z < last) if pack else z == z

    def finish(n, carry):
        def sent(d, carry):
            for h in range(PARTS):
                pl.when((d != z) & dense_sender)(lambda: right_copy(n, d, h).wait_send())
            return carry

        lax.fori_loop(0, depth, sent, 0)
        c_left(n).wait()
        return carry

    def finish_start():
        each_peer(lambda to: map_copy(to, me).wait_send())
        for d in range(depth):
            int_copy(d, core).wait_send()

    def step(t, carry):
        pl.when(t < chunks)(lambda: ladder_step(t))

        m = t - z
        live = (m >= 0) & (m < chunks)
        m_left = t - (last - z)
        live_left = (m_left >= 0) & (m_left < chunks)
        m_last = t - farther
        m_out = m_last - 1
        whole = (m_out >= 0) & (m_out < chunks) & (m_out % s.per_load == s.per_load - 1)

        def unpack(when):
            pl.when((z == 1) & live & when)(lambda: unpack_step(m, True))
            pl.when((z == last - 1) & live_left & when)(lambda: unpack_step(m_left, False))

        if pack:
            unpack(t < chunks)
        pl.when(dense_right & live)(lambda: right_step(m))
        pl.when(dense_left & live_left)(lambda: left_step(m_left))
        pl.when((m_last >= 0) & (m_last < chunks))(lambda: last_step(m_last))
        if pack:
            unpack(t >= chunks)
        pl.when(whole)(lambda: turn_step(m_out // s.per_load))
        pl.when(t == 1)(finish_start)

        @pl.when((t >= LATE) & (t - LATE < chunks))
        def _():
            finish(t - LATE, 0)


        return carry

    lax.fori_loop(0, chunks + depth, step, 0)

    if pack:

        @pl.when(z > 1)
        def _():
            right_spot(spots).wait_recv()
            pl.when(z < last)(lambda: right_spot(right_spots).start())

        @pl.when(z < last - 1)
        def _():
            left_spot(spots).wait_recv()
            pl.when(z > 0)(lambda: left_spot(left_spots).start())

        pl.when(z < last)(lambda: right_spot(spots).wait_send())
        pl.when(z > 0)(lambda: left_spot(spots).wait_send())
        rows = slice(LEAST, LEAST + 8)
        from_left = jnp.where(z == 0, spots[rows, :], right_spots[rows, :])
        from_right = jnp.where(z == last, spots[rows, :], left_spots[rows, :])
        flag_ref[0, 0] = jnp.max(jnp.maximum(from_left, from_right))
        int_map_copy(core).wait_send()

        @pl.when((z == 0) | (z == last))
        def _():
            for n in range(max(0, chunks - 2), chunks):
                packed_left(n)

    else:
        flag_ref[0, 0] = jnp.float32(0)

    lax.fori_loop(max(0, chunks + depth - LATE), chunks, finish, 0)


def residual(s, pack, amplitudes, amp_tiles, occ_coupling, integrals, int_tiles):
    vmem, dma = pltpu.VMEM, pltpu.SemaphoreType.DMA
    any_space = pl.BlockSpec(memory_space=pl.ANY)
    in_vmem = pl.BlockSpec(memory_space=pltpu.VMEM)
    chunks, depth, group = s.chunks, s.depth, s.group
    both = CORES * s.cols
    scratch = [
        vmem((2, s.firsts, s.load, s.cols), BF16),
        vmem((s.slots, s.per_load * group, s.block, s.cols), BF16),
        vmem((chunks, s.rows, both), BF16),
        vmem((s.rows, both), BF16),
        vmem((s.rows, both), BF16),
        vmem(amp_tiles.shape[::-1], jnp.int32),
        vmem(int_tiles.shape, jnp.int32),
        vmem((s.firsts, TILE), F32),
        vmem((s.occ, CORES * TILE), F32),
        vmem((depth, both, s.width), BF16),
        vmem((chunks, depth, s.flat, TILE), BF16),
        vmem((chunks, depth + 1, s.flat, TILE), BF16),
        vmem((s.flat, TILE), F32),
        vmem((chunks, s.rows, s.width), BF16),
        vmem((chunks, group, s.block, s.half), BF16),
        vmem((s.count, s.count), BF16),
        vmem((s.count, s.sub_i * s.occ), BF16),
        vmem((s.rows, s.rows), BF16),
        dma((2,)),
        dma((2,)),
        dma((chunks,)),
        dma((chunks,)),
        dma((group,)),
        dma((group,)),
        dma((depth,)),
        dma((depth,)),
        dma((depth,)),
        dma((chunks, depth * PARTS)),
        dma((chunks, depth * PARTS)),
        dma((chunks, depth * PARTS)),
        dma((chunks,)),
        dma((chunks,)),
    ]
    if pack:
        scratch += [
            vmem((s.sent, s.sent), BF16),
            vmem((2, s.room, TILE), BF16),
            vmem((LEAST + 8, TILE), F32),
            vmem((LEAST + 8, TILE), F32),
            vmem((LEAST + 8, TILE), F32),
            vmem((CORES * (s.cols // TILE), TILE), F32),
            dma((2,)),
            dma(()),
            dma(()),
            dma(()),
            dma(()),
        ]
    return pl.pallas_call(
        functools.partial(residual_kernel, s, pack),
        out_shape=(
            pltpu.VMEM((s.half, s.firsts * s.occ), BF16),
            jax.ShapeDtypeStruct((1, 1), F32),
        ),
        in_specs=[any_space, any_space, in_vmem, any_space, any_space],
        out_specs=(in_vmem, pl.BlockSpec(memory_space=pltpu.SMEM)),
        scratch_shapes=scratch,
        compiler_params=pltpu.CompilerParams(
            collective_id=1 if pack else 0,
            has_side_effects=True,
            vmem_limit_bytes=58 * 1024 * 1024,
        ),
        name="packed" if pack else "dense",
    )(
        amplitudes.reshape(s.firsts, s.occ, s.cols),
        amp_tiles.T,
        occ_coupling,
        integrals,
        int_tiles,
    )


def shards(mesh_shape, *arrays):
    s = Sizes(mesh_shape, arrays[0], arrays[2], arrays[3])
    if PACK and s.can_pack:
        out, used = residual(s, True, *arrays)
        return lax.cond(
            used[0, 0] > s.room, lambda: residual(s, False, *arrays)[0], lambda: out
        )
    return residual(s, False, *arrays)[0]


PACK = True


def solution(mesh):
    shape = mesh.devices.shape
    in_specs = (P("bulk", "cuts"), P("bulk", "cuts"), P(), P("cuts", None), P("cuts", None))
    return jax.shard_map(
        functools.partial(shards, shape),
        mesh=mesh,
        in_specs=in_specs,
        out_specs=P("cuts", "bulk"),
        check_vma=False,
    )
```

```python
import functools

import jax
import jax.numpy as jnp
from jax import lax
from jax.experimental import pallas as pl
from jax.experimental.pallas import tpu as pltpu
from jax.sharding import PartitionSpec as P

TILE = 128
CORES = 2
LEAST = 16
BLOCK = 256
AHEAD = 2
LATE = 5
PARTS = 1
MESH = pl.DeviceIdType.MESH
F32 = jnp.float32
BF16 = jnp.bfloat16


def dot(a, b):
    return jnp.dot(a, b, preferred_element_type=F32)


def iota(shape, axis):
    return lax.broadcasted_iota(jnp.int32, shape, axis)


def one_hot(condition):
    return jnp.where(condition, 1.0, 0.0).astype(BF16)


class Sizes:
    def __init__(self, mesh_shape, amplitudes, occ_coupling, integrals):
        self.bulk, cuts = mesh_shape
        self.depth = cuts // CORES
        self.group = self.bulk * CORES
        local_rows, self.cols = amplitudes.shape
        self.occ = occ_coupling.shape[0]
        self.firsts = local_rows // self.occ
        self.pair = max(1, LEAST // self.firsts)
        self.seconds = self.pair * self.group
        self.chunks = self.occ // self.seconds
        self.load = max(LEAST, self.seconds)
        self.per_load = self.load // self.seconds
        self.loads = self.occ // self.load
        self.slots = 3 if self.per_load > 1 else AHEAD + 2
        self.width = integrals.shape[1] // self.depth
        self.half = self.width // CORES
        self.rows = self.pair * self.occ
        self.block = self.firsts * self.pair
        self.sub_j = min(self.load, max(LEAST, BLOCK // self.firsts))
        self.sub_i = min(self.firsts, BLOCK // self.sub_j)
        self.count = self.sub_i * self.sub_j
        self.tiles = self.width // TILE
        self.flat = self.tiles * self.rows
        self.piece = self.flat // PARTS
        self.sent = (self.depth - 1) * self.flat
        self.can_pack = self.pair == 1 and self.depth == 4 and self.occ == TILE
        self.room = self.sent * 26 // 32 // LEAST * LEAST


def residual_kernel(s, pack, *refs):
    (
        amp_hbm,
        tiles_hbm,
        occ_ref,
        int_hbm,
        int_tiles_hbm,
        turned,
        flag_ref,
        x_buf,
        send_buf,
        slab,
        tau,
        mask,
        tiles_ref,
        int_tiles_ref,
        map_send,
        map_recv,
        ints,
        part,
        inbox,
        acc,
        c_send,
        c_recv,
        split_rows,
        chosen,
        mix,
        x_sem,
        tiles_sem,
        a_send_sem,
        a_recv_sem,
        map_send_sem,
        map_recv_sem,
        int_local_sem,
        int_send_sem,
        int_recv_sem,
        z_send_sem,
        right_sem,
        left_sem,
        c_send_sem,
        c_recv_sem,
    ) = refs[:39]
    if pack:
        (
            choose,
            packed,
            spots,
            right_spots,
            left_spots,
            int_map,
            spot_send_sem,
            right_spot_sem,
            left_spot_sem,
            int_map_send_sem,
            int_map_recv_sem,
        ) = refs[39:]
    depth, group, chunks, cols, pair = s.depth, s.group, s.chunks, s.cols, s.pair
    block, half, flat, piece = s.block, s.half, s.flat, s.piece
    b = lax.axis_index("bulk")
    cut = lax.axis_index("cuts")
    z = cut // CORES
    core = cut % CORES
    me = b * CORES + core
    last = depth - 1

    def aligned(start, size):
        return pl.ds(pl.multiple_of(start, size), size)

    def at_rank(rank):
        return (rank // CORES, z * CORES + rank % CORES)

    def along(zz):
        return (b, zz * CORES + core)

    def remote(src, dst, send_sem, recv_sem, device):
        return pltpu.make_async_remote_copy(
            src_ref=src,
            dst_ref=dst,
            send_sem=send_sem,
            recv_sem=recv_sem,
            device_id=device,
            device_id_type=MESH,
        )

    def each_peer(body):
        def step(k, carry):
            body((me + k) % group)
            return carry

        lax.fori_loop(1, group, step, 0)

    def x_copy(u):
        return pltpu.make_async_copy(
            amp_hbm.at[:, aligned(u * s.load, s.load), :], x_buf.at[u % 2], x_sem.at[u % 2]
        )

    def place(n, rank):
        return slab.at[n, aligned((rank // CORES) * block, block), aligned((rank % CORES) * cols, cols)]

    def outgoing(n, to):
        return send_buf.at[(n // s.per_load) % s.slots, (n % s.per_load) * group + to]

    def a_copy(n, to):
        return remote(
            outgoing(n, to), place(n, me), a_send_sem.at[n], a_recv_sem.at[n], at_rank(to)
        )

    def a_arrived(n):
        return pltpu.make_async_copy(slab.at[n], slab.at[n], a_recv_sem.at[n])

    def a_left(n):
        ref = send_buf.at[(n // s.per_load) % s.slots, pl.ds((n % s.per_load) * group, group - 1)]
        return pltpu.make_async_copy(ref, ref, a_send_sem.at[n])

    def map_place(source):
        return map_recv.at[
            aligned((source // CORES) * s.firsts, s.firsts), aligned((source % CORES) * TILE, TILE)
        ]

    def map_copy(to, source):
        return remote(
            map_send, map_place(source), map_send_sem.at[to], map_recv_sem.at[source], at_rank(to)
        )

    def int_local(d):
        return pltpu.make_async_copy(
            int_hbm.at[:, aligned(d * s.width, s.width)],
            ints.at[d, aligned(core * cols, cols), :],
            int_local_sem.at[d],
        )

    def int_copy(d, source):
        return remote(
            ints.at[d, aligned(core * cols, cols), :],
            ints.at[d, aligned(source * cols, cols), :],
            int_send_sem.at[d],
            int_recv_sem.at[d],
            at_rank(b * CORES + 1 - core),
        )

    def right_copy(n, d, h):
        span = pl.ds(h * piece, piece)
        return remote(
            part.at[n, d, span],
            inbox.at[n, d + 1, span],
            z_send_sem.at[n, d * PARTS + h],
            right_sem.at[n, d * PARTS + h],
            along((z + 1) % depth),
        )

    def left_copy(n, d, h):
        span = pl.ds(h * piece, piece)
        return remote(
            part.at[n, d, span],
            inbox.at[n, d, span],
            z_send_sem.at[n, d * PARTS + h],
            left_sem.at[n, d * PARTS + h],
            along((z + last) % depth),
        )

    def c_copy(n, to):
        return remote(
            c_send.at[n, aligned((to // CORES) * block, block), aligned((to % CORES) * half, half)],
            c_recv.at[n, me],
            c_send_sem.at[n],
            c_recv_sem.at[n],
            at_rank(to),
        )

    def c_own(n):
        return pltpu.make_async_copy(
            c_send.at[n, aligned(b * block, block), aligned(core * half, half)],
            c_recv.at[n, me],
            c_recv_sem.at[n],
        )

    def c_arrived(n):
        return pltpu.make_async_copy(c_recv.at[n], c_recv.at[n], c_recv_sem.at[n])

    def c_left(n):
        ref = c_recv.at[n, pl.ds(0, group - 1)]
        return pltpu.make_async_copy(ref, ref, c_send_sem.at[n])

    def prepare(u):
        x_copy(u).wait()
        for gi in range(s.firsts // s.sub_i):
            for gj in range(s.load // s.sub_j):
                x = x_buf[
                    u % 2,
                    gi * s.sub_i : (gi + 1) * s.sub_i,
                    gj * s.sub_j : (gj + 1) * s.sub_j,
                    :,
                ]
                y = dot(split_rows[...], x.reshape(s.count, cols)).astype(BF16)
                send_buf[
                    u % s.slots,
                    gj * s.sub_j // pair : (gj + 1) * s.sub_j // pair,
                    gi * s.sub_i * pair : (gi + 1) * s.sub_i * pair,
                    :,
                ] = y.reshape(s.sub_j // pair, s.sub_i * pair, cols)
        pl.when(u + 2 < s.loads)(lambda: x_copy(u + 2).start())

    def send_amplitudes(n):
        each_peer(lambda to: a_copy(n, to).start())
        pltpu.make_async_copy(outgoing(n, me), place(n, me), a_recv_sem.at[n]).start()

    def dress(n):
        span = min(512, CORES * cols)
        for at in range(0, CORES * cols, span):
            kept = mask[:, at : at + span]
            masked = slab[n, :, at : at + span] * kept
            mixed = dot(mix[...], masked)
            dressed = (masked.astype(F32) + mixed).astype(BF16)
            tau[:, at : at + span] = dressed * kept

    def in_turn(k):
        return jnp.where(z * 2 < depth, last - k, k)

    tiles_copy = pltpu.make_async_copy(tiles_hbm, tiles_ref, tiles_sem.at[0])
    int_tiles_copy = pltpu.make_async_copy(int_tiles_hbm, int_tiles_ref, tiles_sem.at[1])
    x_copy(0).start()
    tiles_copy.start()
    int_tiles_copy.start()
    barrier = pltpu.get_barrier_semaphore()

    def greet(device):
        pl.semaphore_signal(barrier, inc=1, device_id=device, device_id_type=MESH)

    each_peer(lambda to: greet(at_rank(to)))
    pl.when(z > 0)(lambda: greet(along(z - 1)))
    pl.when(z < last)(lambda: greet(along(z + 1)))
    for k in range(depth):
        int_local(in_turn(k)).start()
    if s.loads > 1:
        x_copy(1).start()

    r, c = iota((s.count, 1), 0), iota((1, s.count), 1)
    natural = ((r // pair) % s.sub_i) * s.sub_j + (r // (pair * s.sub_i)) * pair + r % pair
    split_rows[...] = one_hot(c == natural)
    prepare(0)
    tiles_copy.wait()
    int_tiles_copy.wait()
    kept_tiles = tiles_ref[...].astype(F32)
    kept_tiles = jnp.concatenate(
        [kept_tiles, jnp.zeros((kept_tiles.shape[0], TILE - s.firsts), F32)], axis=1
    )
    kept_tiles = jnp.concatenate(
        [kept_tiles, jnp.zeros((TILE - kept_tiles.shape[0], TILE), F32)], axis=0
    )
    map_send[...] = kept_tiles.T[: s.firsts]
    own_tiles = cols // TILE
    if pack:
        int_tiles = int_tiles_ref[...].astype(F32)
        int_map[aligned(core * own_tiles, own_tiles), :] = jnp.concatenate(
            [int_tiles, jnp.zeros((own_tiles, TILE - int_tiles.shape[1]), F32)], axis=1
        )

    def mask_ints(k):
        d = in_turn(k)
        int_local(d).wait()
        tiles = int_tiles_ref.shape[1]
        spread = one_hot(
            iota((1, s.width), 1) // TILE == iota((tiles, 1), 0) - d * s.tiles
        )
        kept = dot(int_tiles_ref[...].astype(F32).astype(BF16), spread).astype(BF16)
        for j in range(own_tiles):
            span = aligned(core * cols + j * TILE, TILE)
            ints[d, span, :] = ints[d, span, :] * kept[j : j + 1, :]

    mask_ints(0)

    for at in range(0, turned.shape[1], 512):
        turned[:, at : at + 512] = jnp.zeros((half, 512), BF16)

    ends = jnp.where(z > 0, 1, 0) + jnp.where(z < last, 1, 0)
    pl.semaphore_wait(barrier, group - 1 + ends)

    each_peer(lambda to: map_copy(to, me).start())
    own_map = pltpu.make_async_copy(map_send, map_place(me), map_recv_sem.at[me])
    own_map.start()
    if pack:

        def int_map_copy(source):
            span = aligned(source * own_tiles, own_tiles)
            mine = aligned(core * own_tiles, own_tiles)
            return remote(
                int_map.at[mine],
                int_map.at[span],
                int_map_send_sem,
                int_map_recv_sem,
                at_rank(b * CORES + 1 - core),
            )

        int_map_copy(core).start()
    send_amplitudes(0)

    int_copy(in_turn(0), core).start()

    def mask_more(k, carry):
        mask_ints(k)
        int_copy(in_turn(k), core).start()
        return carry

    lax.fori_loop(1, depth, mask_more, 0)
    for n in range(1, min(AHEAD + 1, chunks)):
        if n % s.per_load == 0:
            prepare(n // s.per_load)
        if n < AHEAD:
            send_amplitudes(n)
    tall = one_hot(iota((s.rows, s.occ), 0) // pair == iota((s.rows, s.occ), 1))
    if pair == 1:
        mix[...] = occ_ref[...]
    else:
        wide = one_hot(iota((s.occ, s.rows), 1) // pair == iota((s.occ, s.rows), 0))
        stretched = dot(dot(tall, occ_ref[...]).astype(BF16), wide)
        same = iota((s.rows, s.rows), 0) % pair == iota((s.rows, s.rows), 1) % pair
        mix[...] = jnp.where(same, stretched, 0.0).astype(BF16)

    own_map.wait()
    each_peer(lambda source: map_copy(source, source).wait_recv())
    tiles_all = dot(tall, map_recv[...].astype(BF16)).astype(BF16)
    lane = iota((CORES * TILE, 1), 0)
    col = iota((1, CORES * cols), 1)
    mask[...] = dot(
        tiles_all, one_hot(lane == (col // cols) * TILE + (col % cols) // TILE)
    ).astype(BF16)

    if pack:
        others = (depth - 1) * s.tiles
        room = s.room

        def spot_copy(src, sem, dst, recv, device):
            return remote(src, dst, sem, recv, device)

        def right_spot(src):
            return remote(
                src, right_spots, spot_send_sem.at[0], right_spot_sem, along((z + 1) % depth)
            )

        def left_spot(src):
            return remote(
                src, left_spots, spot_send_sem.at[1], left_spot_sem, along((z + last) % depth)
            )

        int_map_copy(1 - core).wait_recv()

        @pl.when((z == 0) | (z == last))
        def _():
            hits = jnp.zeros((s.occ, TILE), F32)
            for k in range(CORES):
                rows = int_map[k * own_tiles : (k + 1) * own_tiles, :]
                rows = jnp.concatenate([rows, jnp.zeros((TILE - own_tiles, TILE), F32)], axis=0)
                hits += dot(
                    map_recv[:, k * TILE : (k + 1) * TILE].astype(BF16), rows.astype(BF16)
                )
            hits = jnp.where(hits > 0.5, 1.0, 0.0).T
            hits = jnp.where(z == 0, hits[s.tiles : s.tiles + others], hits[:others])
            hits = jnp.concatenate([hits, jnp.zeros((LEAST - others, TILE), F32)], axis=0)
            marks = hits.astype(BF16)
            i, k = iota((TILE, TILE), 0), iota((TILE, TILE), 1)
            ahead = dot(marks, one_hot(i < k))
            totals = dot(marks, jnp.ones((TILE, TILE), BF16))
            r, c = iota((LEAST, LEAST), 0), iota((LEAST, LEAST), 1)
            before = jnp.where(z == 0, one_hot(c > r), one_hot(c < r))
            ahead += dot(before, totals.astype(BF16))
            spots[0:LEAST, :] = jnp.where(hits > 0.5, ahead, -1.0)
            total = jnp.sum(hits, axis=0, keepdims=True)
            total = jnp.sum(total, axis=1, keepdims=True)
            spots[LEAST:, :] = jnp.broadcast_to(total, (spots.shape[0] - LEAST, TILE))
            pl.when(z == 0)(lambda: right_spot(spots).start())
            pl.when(z == last)(lambda: left_spot(spots).start())
            at = iota((room, TILE), 0).astype(F32)
            for k in range(others):
                choose[0:room, k * TILE : (k + 1) * TILE] = one_hot(at == spots[k : k + 1, :])

        def restore(ref):
            where = jnp.concatenate(
                [ref[0:LEAST, :], jnp.full((TILE - LEAST, TILE), -1.0, F32)], axis=0
            ).T
            at = iota((TILE, room), 1).astype(F32)
            for k in range(others):
                choose[k * TILE : (k + 1) * TILE, 0:room] = one_hot(at == where[:, k : k + 1])

        @pl.when(z == 1)
        def _():
            right_spot(spots).wait_recv()
            right_spot(right_spots).start()

        @pl.when(z == last - 1)
        def _():
            left_spot(spots).wait_recv()
            left_spot(left_spots).start()

        pieces = []
        for begin in range(0, room, piece):
            pieces.append((begin, min(room, begin + piece)))

        def packed_copy(n, o, to_right):
            begin, end = pieces[o]
            base = 2 * flat if to_right else 0
            return remote(
                packed.at[n % 2, pl.ds(begin, end - begin), :],
                inbox_rows(n, base + begin, end - begin),
                z_send_sem.at[n, o],
                (right_sem if to_right else left_sem).at[n, o],
                along((z + 1) % depth) if to_right else along((z + last) % depth),
            )

        def inbox_rows(n, begin, size):
            slot = begin // flat
            return inbox.at[n, slot, pl.ds(begin - slot * flat, size), :]

        def packed_left(n):
            for o in range(len(pieces)):
                packed_copy(n, o, True).wait_send()


    farther = jnp.maximum(z, last - z)
    dense_right = (z > 0) if not pack else (z > 1)
    dense_left = (z < last) if not pack else (z < last - 1)

    def add_into(n, d, slot, h):
        rows = slice(h * piece, (h + 1) * piece)
        total = part[n, d, rows, :].astype(F32) + inbox[n, slot, rows, :].astype(F32)
        part[n, d, rows, :] = total.astype(BF16)

    def ladder_step(t):
        a_arrived(t).wait()
        pl.when(t + AHEAD < chunks)(lambda: send_amplitudes(t + AHEAD))
        dress(t)

        def ladder(k, carry):
            d = in_turn(k)
            pl.when(t == 0)(lambda: int_copy(d, 1 - core).wait_recv())
            y = dot(tau[...], ints[d]).astype(BF16)
            for k in range(s.tiles):
                part[t, d, k * s.rows : (k + 1) * s.rows, :] = y[:, k * TILE : (k + 1) * TILE]
            if not pack:
                for h in range(PARTS):
                    pl.when((z == 0) & (d > 0))(lambda: right_copy(t, d, PARTS - 1 - h).start())
                    pl.when((z == last) & (d < last))(lambda: left_copy(t, d, h).start())
            return carry

        lax.fori_loop(0, depth, ladder, 0)
        if pack:

            @pl.when((z == 0) | (z == last))
            def _():
                pl.when(t >= 2)(lambda: packed_left(t - 2))
                first = jnp.where(z == 0, 1, 0)
                x = part[t, pl.ds(first, depth - 1)].reshape(s.sent, TILE)
                for o, (begin, end) in enumerate(pieces):
                    if begin % flat == 0:
                        until = min(room, begin + flat)
                        packed[t % 2, begin:until, :] = dot(choose[begin:until, :], x).astype(BF16)
                    pl.when(z == 0)(lambda: packed_copy(t, o, True).start())
                    pl.when(z == last)(lambda: packed_copy(t, o, False).start())

        a_left(t).wait()

        if pack:

            @pl.when(t == 0)
            def _():
                pl.when(z == 1)(lambda: restore(right_spots))
                pl.when(z == last - 1)(lambda: restore(left_spots))

        ready = t + AHEAD + 1
        pl.when((ready < chunks) & (ready % s.per_load == 0))(
            lambda: prepare(ready // s.per_load)
        )

    def unpack_step(m, to_right):
        base = 2 if to_right else 0
        count = (depth - 1) * PARTS
        x = []
        for o in range(count):
            if o < len(pieces):
                packed_copy(m, o, to_right).wait_recv()
                begin, end = pieces[o]
                rows = slice(begin % flat, begin % flat + end - begin)
                x.append(inbox[m, base + begin // flat, rows, :])
            g = count - 1 - o if to_right else o
            d, h = g // PARTS + (1 if to_right else 0), g % PARTS
            y = dot(choose[g * piece : (g + 1) * piece, :end], jnp.concatenate(x, axis=0))
            rows = slice(h * piece, (h + 1) * piece)
            part[m, d, rows, :] = (part[m, d, rows, :].astype(F32) + y).astype(BF16)
            if to_right and d > 1:
                right_copy(m, d, h).start()
            if not to_right and d < depth - 2:
                left_copy(m, d, h).start()

    def right_step(m):
        def pass_on(k, carry):
            d = last - k
            for h in reversed(range(PARTS)):
                right_copy(m, d, h).wait_recv()
                add_into(m, d, d + 1, h)
                right_copy(m, d, h).start()
            return carry

        lax.fori_loop(0, last - z, pass_on, 0)

    def left_step(m):
        def pass_on(d, carry):
            for h in range(PARTS):
                left_copy(m, d, h).wait_recv()
                add_into(m, d, d, h)
                left_copy(m, d, h).start()
            return carry

        lax.fori_loop(0, z, pass_on, 0)

    def last_step(m):
        acc[...] = part[m, z].astype(F32)

        @pl.when(dense_right)
        def _():
            for h in range(PARTS):
                right_copy(m, z, h).wait_recv()
            acc[...] += inbox[m, z + 1].astype(F32)

        @pl.when(dense_left)
        def _():
            for h in range(PARTS):
                left_copy(m, z, h).wait_recv()
            acc[...] += inbox[m, z].astype(F32)

        for k in range(s.tiles):
            c_send[m, :, k * TILE : (k + 1) * TILE] = acc[k * s.rows : (k + 1) * s.rows, :].astype(
                BF16
            )
        each_peer(lambda to: c_copy(m, to).start())
        c_own(m).start()

    def turn_step(u):
        span = s.sub_i * s.occ
        r = iota((s.count, 1), 0)
        spot = ((r // pair) % s.sub_i) * s.occ + (r // (pair * s.sub_i)) * pair + r % pair
        per = s.sub_j // pair
        for gj in range(s.load // s.sub_j):
            shift = u * s.load + gj * s.sub_j
            chosen[...] = one_hot(iota((1, span), 1) - shift == spot)
            if gj == 0:
                for k in range(s.per_load):
                    c_arrived(u * s.per_load + k).wait()
            for gi in range(s.firsts // s.sub_i):
                pieces = []
                begin = gj * per
                while begin < (gj + 1) * per:
                    end = min((gj + 1) * per, (begin // group + 1) * group)
                    k = begin // group
                    pieces.append(
                        c_recv[
                            u * s.per_load + k,
                            begin - k * group : end - k * group,
                            gi * s.sub_i * pair : (gi + 1) * s.sub_i * pair,
                            :,
                        ]
                    )
                    begin = end
                x = jnp.concatenate(pieces, axis=0) if len(pieces) > 1 else pieces[0]
                x = x.reshape(s.count, half).T
                step = min(512, span)
                for at in range(0, span, step):
                    y = dot(x, chosen[:, at : at + step]).astype(BF16)
                    cols_at = gi * span + at
                    turned[:, cols_at : cols_at + step] = turned[:, cols_at : cols_at + step] + y

    dense_sender = (z > 0) & (z < last) if pack else z == z

    def finish(n, carry):
        def sent(d, carry):
            for h in range(PARTS):
                pl.when((d != z) & dense_sender)(lambda: right_copy(n, d, h).wait_send())
            return carry

        lax.fori_loop(0, depth, sent, 0)
        c_left(n).wait()
        return carry

    def finish_start():
        each_peer(lambda to: map_copy(to, me).wait_send())
        for d in range(depth):
            int_copy(d, core).wait_send()

    def step(t, carry):
        pl.when(t < chunks)(lambda: ladder_step(t))

        m = t - z
        live = (m >= 0) & (m < chunks)
        m_left = t - (last - z)
        live_left = (m_left >= 0) & (m_left < chunks)
        m_last = t - farther
        m_out = m_last - 1
        whole = (m_out >= 0) & (m_out < chunks) & (m_out % s.per_load == s.per_load - 1)

        def unpack(when):
            pl.when((z == 1) & live & when)(lambda: unpack_step(m, True))
            pl.when((z == last - 1) & live_left & when)(lambda: unpack_step(m_left, False))

        if pack:
            unpack(t < chunks)
        pl.when(dense_right & live)(lambda: right_step(m))
        pl.when(dense_left & live_left)(lambda: left_step(m_left))
        pl.when((m_last >= 0) & (m_last < chunks))(lambda: last_step(m_last))
        if pack:
            unpack(t >= chunks)
        pl.when(whole)(lambda: turn_step(m_out // s.per_load))
        pl.when(t == 1)(finish_start)

        @pl.when((t >= LATE) & (t - LATE < chunks))
        def _():
            finish(t - LATE, 0)


        return carry

    lax.fori_loop(0, chunks + depth, step, 0)

    if pack:

        @pl.when(z > 1)
        def _():
            right_spot(spots).wait_recv()
            pl.when(z < last)(lambda: right_spot(right_spots).start())

        @pl.when(z < last - 1)
        def _():
            left_spot(spots).wait_recv()
            pl.when(z > 0)(lambda: left_spot(left_spots).start())

        pl.when(z < last)(lambda: right_spot(spots).wait_send())
        pl.when(z > 0)(lambda: left_spot(spots).wait_send())
        rows = slice(LEAST, LEAST + 8)
        from_left = jnp.where(z == 0, spots[rows, :], right_spots[rows, :])
        from_right = jnp.where(z == last, spots[rows, :], left_spots[rows, :])
        flag_ref[0, 0] = jnp.max(jnp.maximum(from_left, from_right))
        int_map_copy(core).wait_send()

        @pl.when((z == 0) | (z == last))
        def _():
            for n in range(max(0, chunks - 2), chunks):
                packed_left(n)

    else:
        flag_ref[0, 0] = jnp.float32(0)

    lax.fori_loop(max(0, chunks + depth - LATE), chunks, finish, 0)


def residual(s, pack, amplitudes, amp_tiles, occ_coupling, integrals, int_tiles):
    vmem, dma = pltpu.VMEM, pltpu.SemaphoreType.DMA
    any_space = pl.BlockSpec(memory_space=pl.ANY)
    in_vmem = pl.BlockSpec(memory_space=pltpu.VMEM)
    chunks, depth, group = s.chunks, s.depth, s.group
    both = CORES * s.cols
    scratch = [
        vmem((2, s.firsts, s.load, s.cols), BF16),
        vmem((s.slots, s.per_load * group, s.block, s.cols), BF16),
        vmem((chunks, s.rows, both), BF16),
        vmem((s.rows, both), BF16),
        vmem((s.rows, both), BF16),
        vmem(amp_tiles.shape[::-1], jnp.int32),
        vmem(int_tiles.shape, jnp.int32),
        vmem((s.firsts, TILE), F32),
        vmem((s.occ, CORES * TILE), F32),
        vmem((depth, both, s.width), BF16),
        vmem((chunks, depth, s.flat, TILE), BF16),
        vmem((chunks, depth + 1, s.flat, TILE), BF16),
        vmem((s.flat, TILE), F32),
        vmem((chunks, s.rows, s.width), BF16),
        vmem((chunks, group, s.block, s.half), BF16),
        vmem((s.count, s.count), BF16),
        vmem((s.count, s.sub_i * s.occ), BF16),
        vmem((s.rows, s.rows), BF16),
        dma((2,)),
        dma((2,)),
        dma((chunks,)),
        dma((chunks,)),
        dma((group,)),
        dma((group,)),
        dma((depth,)),
        dma((depth,)),
        dma((depth,)),
        dma((chunks, depth * PARTS)),
        dma((chunks, depth * PARTS)),
        dma((chunks, depth * PARTS)),
        dma((chunks,)),
        dma((chunks,)),
    ]
    if pack:
        scratch += [
            vmem((s.sent, s.sent), BF16),
            vmem((2, s.room, TILE), BF16),
            vmem((LEAST + 8, TILE), F32),
            vmem((LEAST + 8, TILE), F32),
            vmem((LEAST + 8, TILE), F32),
            vmem((CORES * (s.cols // TILE), TILE), F32),
            dma((2,)),
            dma(()),
            dma(()),
            dma(()),
            dma(()),
        ]
    return pl.pallas_call(
        functools.partial(residual_kernel, s, pack),
        out_shape=(
            pltpu.VMEM((s.half, s.firsts * s.occ), BF16),
            jax.ShapeDtypeStruct((1, 1), F32),
        ),
        in_specs=[any_space, any_space, in_vmem, any_space, any_space],
        out_specs=(in_vmem, pl.BlockSpec(memory_space=pltpu.SMEM)),
        scratch_shapes=scratch,
        compiler_params=pltpu.CompilerParams(
            collective_id=1 if pack else 0,
            has_side_effects=True,
            vmem_limit_bytes=58 * 1024 * 1024,
        ),
        name="packed" if pack else "dense",
    )(
        amplitudes.reshape(s.firsts, s.occ, s.cols),
        amp_tiles.T,
        occ_coupling,
        integrals,
        int_tiles,
    )


def shards(mesh_shape, *arrays):
    s = Sizes(mesh_shape, arrays[0], arrays[2], arrays[3])
    if PACK and s.can_pack:
        out, used = residual(s, True, *arrays)
        return lax.cond(
            used[0, 0] > s.room, lambda: residual(s, False, *arrays)[0], lambda: out
        )
    return residual(s, False, *arrays)[0]


PACK = True


def solution(mesh):
    shape = mesh.devices.shape
    in_specs = (P("bulk", "cuts"), P("bulk", "cuts"), P(), P("cuts", None), P("cuts", None))
    return jax.shard_map(
        functools.partial(shards, shape),
        mesh=mesh,
        in_specs=in_specs,
        out_specs=P("cuts", "bulk"),
        check_vma=False,
    )
```
